32 devices in a mesh: groups: 2 (over x), seq: 16 (over z, y, core).
Axes of the slice: x: 2, y: 2, z: 4, core: 2. Of those that a mesh axis runs over, the one named last changes fastest.
Arguments:
- queries: bfloat16 [128, 8192], P(('groups', 'seq')), parts along dimension 0, may hold values from -15 to 15
- draft_keys: bfloat16 [128, 1024], P(('groups', 'seq')), parts along dimension 0, may hold values from -16 to 16
- draft_values: bfloat16 [128, 1024], P(('groups', 'seq')), parts along dimension 0, may hold values from -6 to 6
- parents: int32 [128], P(('groups', 'seq')), parts along dimension 0, may hold values from -1 to 2, as said below
- private_keys: bfloat16 [32, 1024, 1024], P(('groups', 'seq')), parts along dimension 0, may hold values from -8 to 8
- private_values: bfloat16 [32, 1024, 1024], P(('groups', 'seq')), parts along dimension 0, may hold values from -6 to 6
- priv_lengths: int32 [32], P(('groups', 'seq')), parts along dimension 0, may hold values from 1 to 1024, as said below
- prefix_keys: bfloat16 [32, 16384, 128], P(('groups', 'seq')), parts along dimension 0, may hold values from -8 to 8
- prefix_values: bfloat16 [32, 16384, 128], P(('groups', 'seq')), parts along dimension 0, may hold values from -6 to 6
- out_weight: bfloat16 [8192, 8192], P(None, 'seq'), may hold values from -0.0625 to 0.0625
Outputs:
- output: float32 [128, 8192], P(('groups', 'seq')), parts along dimension 0
The draws below stay inside these ranges and needn't reach their ends.
There are 2 independent parts, one for each index of `groups`. The reference program is written for one: setup_inputs(seed, part) draws one part's arguments, and reference() takes and returns one part's arrays. A program takes and returns all parts, laid end to end along the dimension named above; an argument that names none is the same for every part. Nothing has to cross between parts.
Inputs may be any that keep to these rules, and one draw needn't show every extreme that they name: parents[r * 4 + i] is the draft of request r that draft i extends, always smaller than i; -1 means draft i extends the cached context directly. Request r's live private slots are its first priv_lengths[r] slots; some request has all 1024.
All inputs are finite; a program needn't handle non-finite values.
Results may differ from the reference program's by a relative error of at most 0.0034.
Values may be sent and summed in bfloat16 or wider, within the bound.
No kernel may reach another device: no remote copies, remote signals or barrier semaphores. Data moves between devices by JAX's collectives and lax.ppermute only.
A program may use at most 192 MiB of HBM per device.

```python
import jax
import jax.numpy as jnp
from jax import lax

D = 8192
HEADS = 64
KVH = 8
HD = 128
DRAFT = 4
PRIV = 1024
NBLK = 2
BLOCK = 16384
PREFIX = 32768
REQ = 16
ROWS = 64


def draw_queries(key, part):
    base_draw = jnp.clip(2.5 * jax.random.normal(jax.random.fold_in(key, 1), (ROWS, HEADS * HD), jnp.float32), -15.0, 15.0)
    return base_draw.astype(jnp.bfloat16)


def draw_prefix_keys(key, part):
    base_draw = jnp.clip(jax.random.normal(jax.random.fold_in(key, 2), (KVH * NBLK, BLOCK, HD), jnp.float32), -8.0, 8.0)
    return base_draw.astype(jnp.bfloat16)


def draw_parents(key, part):
    within = jnp.arange(ROWS, dtype=jnp.int32) % DRAFT
    picked = jax.random.randint(jax.random.fold_in(key, 3), (ROWS,), 0, DRAFT * 12)
    chosen = (picked % (within + 1) - 1).astype(jnp.int32)
    chain = (within - 1).astype(jnp.int32)
    return jnp.where(jnp.arange(ROWS, dtype=jnp.int32) < DRAFT, chain, chosen).astype(jnp.int32)


def draw_priv_lengths(key, part):
    lengths = jax.random.randint(jax.random.fold_in(key, 4), (REQ,), 1, PRIV + 1)
    longest = jax.random.randint(jax.random.fold_in(key, 5), (), 0, REQ)
    return lengths.at[longest].set(PRIV).astype(jnp.int32)


def block_levels(key, dims, cuts, smallest, largest):
    def one(axis_at, parts):
        heights = jax.random.uniform(jax.random.fold_in(jax.random.fold_in(key, 6), axis_at), (parts,), jnp.float32, smallest / len(cuts), largest / len(cuts))
        return jnp.repeat(jnp.exp(heights), dims[axis_at] // parts).reshape((-1,) + (1,) * (len(dims) - axis_at - 1))

    level = one(*cuts[0])
    for cut in cuts[1:]:
        level = level * one(*cut)
    return level


def normal_values(own_key, shape, spread, bound, shards=(), kind=jnp.bfloat16):
    entries = jax.random.normal(own_key, shape, jnp.float32) * spread
    if len(shards) > 0:
        entries = block_levels(own_key, shape, shards, -0.22, 0.18) * entries
    return jnp.clip(entries, min=-bound, max=bound).astype(kind)


def setup_inputs(seed: int = 0, part: int = 0) -> dict:
    streams_of = jax.random.split(jax.random.key(seed), 11)
    part_keys = jax.random.split(jax.random.fold_in(streams_of[10], part), 11)
    queries = draw_queries(jax.random.fold_in(jax.random.fold_in(streams_of[10], part), 71), part)
    draft_keys = normal_values(part_keys[1], (ROWS, KVH * HD), 3.0, 16.0, ((0, 16),))
    draft_values = normal_values(part_keys[2], (ROWS, KVH * HD), 1.0, 6.0, ((0, 16),))
    parents = draw_parents(jax.random.fold_in(jax.random.fold_in(streams_of[10], part), 71), part)
    private_keys = normal_values(part_keys[4], (REQ, PRIV, KVH * HD), 1.3, 8.0, ((0, 16),))
    private_values = normal_values(part_keys[5], (REQ, PRIV, KVH * HD), 1.0, 6.0, ((0, 16),))
    priv_lengths = draw_priv_lengths(jax.random.fold_in(jax.random.fold_in(streams_of[10], part), 71), part)
    prefix_keys = draw_prefix_keys(jax.random.fold_in(jax.random.fold_in(streams_of[10], part), 71), part)
    prefix_values = normal_values(part_keys[8], (KVH * NBLK, BLOCK, HD), 1.0, 6.0, ((0, 16),))
    out_weight = normal_values(streams_of[9], (HEADS * HD, D), (HEADS * HD) ** -0.5, 0.0625, ((1, 16),))
    return {"queries": queries, "draft_keys": draft_keys, "draft_values": draft_values, "parents": parents, "private_keys": private_keys, "private_values": private_values, "priv_lengths": priv_lengths, "prefix_keys": prefix_keys, "prefix_values": prefix_values, "out_weight": out_weight}


def tree_visible(parents):
    parent_rows = parents.reshape(-1, DRAFT).astype(jnp.int32)
    positions = jnp.arange(DRAFT, dtype=jnp.int32)
    visible = jnp.broadcast_to(positions[:, None] == positions[None, :], (parent_rows.shape[0], DRAFT, DRAFT))
    ancestor = parent_rows
    for repeat_step in range(DRAFT - 1):
        matched = ancestor[:, :, None] == positions[None, None, :]
        visible = visible | matched
        lifted = jnp.sum(jnp.where(matched, parent_rows[:, None, :], 0), axis=2).astype(jnp.int32)
        ancestor = jnp.where(ancestor >= 0, lifted, -1).astype(jnp.int32)
    return visible


def rounded(weights):
    return lax.optimization_barrier(weights.astype(jnp.bfloat16)).astype(jnp.float32)


def reference(queries, draft_keys, draft_values, parents, private_keys, private_values, priv_lengths, prefix_keys, prefix_values, out_weight):
    group_heads = HEADS // KVH
    score_scale = HD ** -0.5
    visible = tree_visible(parents)
    live_slots = jnp.arange(PRIV, dtype=jnp.int32)[None, :] < priv_lengths[:, None]
    key_heads = prefix_keys.reshape(KVH, PREFIX, HD)
    value_heads = prefix_values.reshape(KVH, PREFIX, HD)

    def one_group(group):
        query_cols = lax.dynamic_slice_in_dim(queries, group * (group_heads * HD), group_heads * HD, 1)
        flat_query = query_cols.reshape(ROWS * group_heads, HD)
        pre_keys = lax.dynamic_index_in_dim(key_heads, group, 0, keepdims=False)
        pre_vals = lax.dynamic_index_in_dim(value_heads, group, 0, keepdims=False)
        pre_scores = jnp.dot(flat_query, pre_keys.T, preferred_element_type=jnp.float32) * score_scale
        pre_scores = pre_scores.reshape(REQ, DRAFT, group_heads, PREFIX)
        query_four = query_cols.reshape(REQ, DRAFT, group_heads, HD).astype(jnp.float32)
        priv_keys = lax.dynamic_slice_in_dim(private_keys, group * HD, HD, 2).astype(jnp.float32)
        priv_vals = lax.dynamic_slice_in_dim(private_values, group * HD, HD, 2).astype(jnp.float32)
        draft_key = lax.dynamic_slice_in_dim(draft_keys, group * HD, HD, 1).reshape(REQ, DRAFT, HD).astype(jnp.float32)
        draft_val = lax.dynamic_slice_in_dim(draft_values, group * HD, HD, 1).reshape(REQ, DRAFT, HD).astype(jnp.float32)
        priv_scores = jnp.einsum('rihd,rkd->rihk', query_four, priv_keys) * score_scale
        priv_scores = jnp.where(live_slots[:, None, None, :], priv_scores, -1e30)
        tree_scores = jnp.einsum('rihd,rjd->rihj', query_four, draft_key) * score_scale
        tree_scores = jnp.where(visible[:, :, None, :], tree_scores, -1e30)
        row_max = jnp.maximum(jnp.max(pre_scores, axis=-1), jnp.maximum(jnp.max(priv_scores, axis=-1), jnp.max(tree_scores, axis=-1)))
        pre_w = jnp.exp(pre_scores - row_max[..., None])
        priv_w = jnp.exp(priv_scores - row_max[..., None])
        tree_w = jnp.exp(tree_scores - row_max[..., None])
        weight_sum = jnp.sum(pre_w, axis=-1) + jnp.sum(priv_w, axis=-1) + jnp.sum(tree_w, axis=-1)
        pre_mix = jnp.dot(pre_w.astype(jnp.bfloat16).reshape(ROWS * group_heads, PREFIX), pre_vals, preferred_element_type=jnp.float32)
        mixture = pre_mix.reshape(REQ, DRAFT, group_heads, HD)
        mixture = mixture + jnp.einsum('rihk,rkd->rihd', rounded(priv_w), priv_vals)
        mixture = mixture + jnp.einsum('rihj,rjd->rihd', rounded(tree_w), draft_val)
        return mixture / weight_sum[..., None]

    per_group = lax.map(one_group, jnp.arange(KVH, dtype=jnp.int32))
    attention = jnp.transpose(per_group, (1, 2, 0, 3, 4)).reshape(ROWS, HEADS * HD).astype(jnp.bfloat16)
    return jnp.dot(attention, out_weight, preferred_element_type=jnp.float32)
```

```python
import functools

import jax
import jax.numpy as jnp
from jax import lax
from jax.experimental import pallas as pl
from jax.experimental.pallas import tpu as pltpu
from jax.sharding import PartitionSpec as P

HEADS = 64
KVH = 8
HD = 128
GROUP = HEADS // KVH
SCALE = HD ** (-0.5)
LOG2E = 1.4426950408889634
LANES = 128
NEG = -1e30
NT = (((1,), (1,)), ((), ()))
F32 = jnp.float32
BF16 = jnp.bfloat16


def private_kernel(par_ref, len_ref, q_ref, dk_ref, dv_ref, k_ref, v_ref, out_ref, *, draft, blocks):
    heads = GROUP // blocks
    rows = GROUP * draft
    slots = k_ref.shape[1]
    q32 = q_ref[...].astype(F32)
    query = jnp.concatenate(
        [q32[:, h * HD : (h + 1) * HD] for h in range(GROUP)], axis=0
    ).astype(BF16)
    live = lax.broadcasted_iota(jnp.int32, (rows, slots), 1) < len_ref[0]
    scores = lax.dot_general(query, k_ref[0], NT, preferred_element_type=F32) * SCALE
    scores = jnp.where(live, scores, NEG)
    seen = []
    for i in range(draft):
        bits = jnp.int32(1 << i)
        for j in range(i):
            bits = bits | jnp.where(par_ref[i] == j, seen[j], 0)
        seen.append(bits)
    row = lax.broadcasted_iota(jnp.int32, (rows, LANES), 0) % draft
    lane = lax.broadcasted_iota(jnp.int32, (rows, LANES), 1)
    shown = lane < 0
    for i in range(draft):
        for j in range(i + 1):
            hit = (seen[i] >> j) & 1
            shown = shown | ((row == i) & (lane == j) & (hit == 1))
    fill = jnp.zeros((LANES - draft, HD), F32)
    dkey = jnp.concatenate([dk_ref[...].astype(F32), fill], axis=0).astype(BF16)
    dval = jnp.concatenate([dv_ref[...].astype(F32), fill], axis=0).astype(BF16)
    tree = lax.dot_general(query, dkey, NT, preferred_element_type=F32) * SCALE
    tree = jnp.where(shown, tree, NEG)
    peak = jnp.maximum(
        jnp.max(scores, axis=1, keepdims=True), jnp.max(tree, axis=1, keepdims=True)
    )
    weights = jnp.exp(scores - peak)
    tree_w = jnp.exp(tree - peak)
    denom = jnp.sum(weights, axis=1, keepdims=True) + jnp.sum(tree_w, axis=1, keepdims=True)
    mixture = jnp.dot(weights.astype(BF16), v_ref[0], preferred_element_type=F32)
    mixture = mixture + jnp.dot(tree_w.astype(BF16), dval, preferred_element_type=F32)
    mixture = mixture / denom
    lse = peak + jnp.log(denom)
    first = lse.astype(BF16).astype(F32)
    second = (lse - first).astype(BF16).astype(F32)
    third = lse - first - second
    stat_lane = lax.broadcasted_iota(jnp.int32, (draft, LANES), 1)
    for b in range(blocks):
        stats = jnp.zeros((draft, LANES), F32)
        for hh in range(heads):
            lo = (b * heads + hh) * draft
            out_ref[b, :, hh * HD : (hh + 1) * HD] = mixture[lo : lo + draft].astype(BF16)
            for t, term in enumerate((first, second, third)):
                stats = jnp.where(stat_lane == 3 * hh + t, term[lo : lo + draft], stats)
        out_ref[b, :, heads * HD :] = stats.astype(BF16)


def private_part(parents, lengths, queries, dkeys, dvals, pkeys, pvals, blocks):
    draft = queries.shape[0]
    slots = pkeys.shape[1]
    wide = (GROUP // blocks) * HD + LANES
    smem = pl.BlockSpec(memory_space=pltpu.SMEM)
    return pl.pallas_call(
        functools.partial(private_kernel, draft=draft, blocks=blocks),
        grid=(KVH,),
        in_specs=[
            smem,
            smem,
            pl.BlockSpec((draft, GROUP * HD), lambda g: (0, g)),
            pl.BlockSpec((draft, HD), lambda g: (0, g)),
            pl.BlockSpec((draft, HD), lambda g: (0, g)),
            pl.BlockSpec((1, slots, HD), lambda g: (0, 0, g)),
            pl.BlockSpec((1, slots, HD), lambda g: (0, 0, g)),
        ],
        out_specs=pl.BlockSpec((blocks, draft, wide), lambda g: (g, 0, 0)),
        out_shape=jax.ShapeDtypeStruct((KVH * blocks, draft, wide), BF16),
        name="private_part",
    )(parents, lengths, queries, dkeys, dvals, pkeys, pvals)


def prefix_kernel(rank_ref, q_ref, k_ref, v_ref, keep_ref, send_ref, q32, qs, peak, denom, acc):
    step = pl.program_id(0)
    owners, draft, _ = q_ref.shape
    rows = owners * draft

    @pl.when(step == 0)
    def _():
        for s in range(owners):
            q32[s * draft : (s + 1) * draft, :] = q_ref[s].astype(F32)
        for h in range(GROUP):
            qs[h * rows : (h + 1) * rows, :] = q32[:, h * HD : (h + 1) * HD].astype(BF16)
        peak[...] = jnp.full(peak.shape, NEG, F32)
        denom[...] = jnp.zeros(denom.shape, F32)
        acc[...] = jnp.zeros(acc.shape, F32)

    scores = lax.dot_general(qs[...], k_ref[0], NT, preferred_element_type=F32)
    tiles = scores.shape[1] // LANES
    top = scores[:, :LANES]
    for j in range(1, tiles):
        top = jnp.maximum(top, scores[:, j * LANES : (j + 1) * LANES])
    old = peak[...]
    new = jnp.maximum(old, jnp.max(top, axis=1, keepdims=True) * (SCALE * LOG2E))
    fade = jnp.exp2(old - new)
    peak[...] = new
    parts = [
        jnp.exp2(scores[:, j * LANES : (j + 1) * LANES] * (SCALE * LOG2E) - new)
        for j in range(tiles)
    ]
    total = parts[0]
    for part in parts[1:]:
        total = total + part
    denom[...] = denom[...] * fade + total
    weights = jnp.concatenate([part.astype(BF16) for part in parts], axis=1)
    acc[...] = acc[...] * fade + jnp.dot(weights, v_ref[0], preferred_element_type=F32)

    @pl.when(step == pl.num_programs(0) - 1)
    def _():
        total = jnp.sum(denom[...], axis=1, keepdims=True)
        acc[...] = acc[...] / total
        denom[...] = peak[...] * (1.0 / LOG2E) + jnp.log(total)
        half = keep_ref.shape[0]
        mine = pl.multiple_of(rank_ref[0] * half, half)
        other = pl.multiple_of((1 - rank_ref[0]) * half, half)
        keep_ref[:, :HD] = acc[pl.ds(mine, half), :]
        keep_ref[:, HD:] = denom[pl.ds(mine, half), :]
        send_ref[:, :HD] = acc[pl.ds(other, half), :]
        send_ref[:, HD:] = denom[pl.ds(other, half), :]


def prefix_part(side, queries, keys, values, span):
    owners, draft, _ = queries.shape
    rows = owners * draft * GROUP
    shape = jax.ShapeDtypeStruct((rows // 2, HD + LANES), F32)
    return pl.pallas_call(
        prefix_kernel,
        grid_spec=pltpu.PrefetchScalarGridSpec(
            num_scalar_prefetch=1,
            grid=(keys.shape[1] // span,),
            in_specs=[
                pl.BlockSpec(queries.shape, lambda i, r: (0, 0, 0)),
                pl.BlockSpec((1, span, HD), lambda i, r: (0, i, 0)),
                pl.BlockSpec((1, span, HD), lambda i, r: (0, i, 0)),
            ],
            out_specs=[
                pl.BlockSpec((rows // 2, HD + LANES), lambda i, r: (0, 0)),
                pl.BlockSpec((rows // 2, HD + LANES), lambda i, r: (0, 0)),
            ],
            scratch_shapes=[
                pltpu.VMEM((owners * draft, GROUP * HD), F32),
                pltpu.VMEM((rows, HD), BF16),
                pltpu.VMEM((rows, LANES), F32),
                pltpu.VMEM((rows, LANES), F32),
                pltpu.VMEM((rows, HD), F32),
            ],
        ),
        out_shape=[shape, shape],
        name="prefix_part",
    )(side, queries, keys, values)


def join(first, second):
    out_a, lse_a = first[:, :HD], first[:, HD:]
    out_b, lse_b = second[:, :HD], second[:, HD:]
    top = jnp.maximum(lse_a, lse_b)
    scale_a = jnp.exp(lse_a - top)
    scale_b = jnp.exp(lse_b - top)
    both = scale_a + scale_b
    return jnp.concatenate(
        [(scale_a * out_a + scale_b * out_b) / both, top + jnp.log(both)], axis=1
    )


def merge_kernel(mine_ref, other_ref, priv_ref, att_ref, p32):
    owners, draft, wide = priv_ref.shape
    rows = owners * draft
    heads = (wide - LANES) // HD
    for s in range(owners):
        p32[s * draft : (s + 1) * draft, :] = priv_ref[s].astype(F32)
    for h in range(heads):
        part = slice(h * rows, (h + 1) * rows)
        col = heads * HD + 3 * h
        lse_p = (p32[:, col : col + 1] + p32[:, col + 1 : col + 2]) + p32[:, col + 2 : col + 3]
        lse_a = mine_ref[part, HD:]
        lse_b = other_ref[part, HD:]
        top = jnp.maximum(jnp.maximum(lse_a, lse_b), lse_p)
        scale_a = jnp.exp(lse_a - top)
        scale_b = jnp.exp(lse_b - top)
        scale_p = jnp.exp(lse_p - top)
        mixed = (
            scale_a * mine_ref[part, :HD]
            + scale_b * other_ref[part, :HD]
            + scale_p * p32[:, h * HD : (h + 1) * HD]
        ) / (scale_a + scale_b + scale_p)
        mixed = mixed.astype(BF16)
        for copy in range(att_ref.shape[0]):
            att_ref[copy, :, h * HD : (h + 1) * HD] = mixed


def merge_part(mine, other, priv, copies):
    owners, draft, wide = priv.shape
    return pl.pallas_call(
        merge_kernel,
        out_shape=jax.ShapeDtypeStruct((copies, owners * draft, wide - LANES), BF16),
        scratch_shapes=[pltpu.VMEM((owners * draft, wide), F32)],
        name="merge_part",
    )(mine, other, priv)


def project_kernel(side_ref, own_ref, oth_ref, wo_ref, wp_ref, out_ref):
    step = pl.program_id(0)
    part = jnp.dot(own_ref[0], wo_ref[0, 0], preferred_element_type=F32)
    part = part + jnp.dot(oth_ref[0], wp_ref[0, 0], preferred_element_type=F32)

    @pl.when(step == 0)
    def _():
        out_ref[...] = part

    @pl.when(step > 0)
    def _():
        out_ref[...] = out_ref[...] + part


def project(side, own, oth, weight):
    chips, rows, deep = own.shape
    cols = weight.shape[1]
    split = weight.reshape(chips, 2, deep, cols)
    return pl.pallas_call(
        project_kernel,
        grid_spec=pltpu.PrefetchScalarGridSpec(
            num_scalar_prefetch=1,
            grid=(chips,),
            in_specs=[
                pl.BlockSpec((1, rows, deep), lambda i, r: (i, 0, 0)),
                pl.BlockSpec((1, rows, deep), lambda i, r: (i, 0, 0)),
                pl.BlockSpec((1, 1, deep, cols), lambda i, r: (i, r[0], 0, 0)),
                pl.BlockSpec((1, 1, deep, cols), lambda i, r: (i, 1 - r[0], 0, 0)),
            ],
            out_specs=pl.BlockSpec((rows, cols), lambda i, r: (0, 0)),
        ),
        out_shape=jax.ShapeDtypeStruct((rows, cols), F32),
        name="project",
    )(side, own, oth, split, split)


def shards(
    queries,
    draft_keys,
    draft_values,
    parents,
    private_keys,
    private_values,
    priv_lengths,
    prefix_keys,
    prefix_values,
    out_weight,
):
    own_rows = queries.shape[0]
    seq = lax.axis_size("seq")
    blocks = seq // KVH
    device = lax.axis_index("seq")
    rank = device % blocks
    top_bit = blocks.bit_length() - 2
    side = ((rank >> top_bit) & 1).astype(jnp.int32).reshape(1)
    parity = (device % 2).astype(jnp.int32).reshape(1)

    def from_partner(array, bit):
        return lax.ppermute(array, "seq", [(i, i ^ 1 << bit) for i in range(seq)])

    by_group = queries.reshape(own_rows, KVH, GROUP * HD).transpose(1, 0, 2)
    ask = jnp.broadcast_to(by_group[:, None], (KVH, blocks, own_rows, GROUP * HD))
    ask = ask.reshape(seq, own_rows, GROUP * HD)
    every_query = lax.all_to_all(ask, "seq", split_axis=0, concat_axis=0, tiled=True)

    told = private_part(
        parents, priv_lengths, queries, draft_keys, draft_values, private_keys, private_values, blocks
    )
    priv = lax.all_to_all(told, "seq", split_axis=0, concat_axis=0, tiled=True)

    span = min(1024, prefix_keys.shape[1])
    mine, gone = prefix_part(side, every_query, prefix_keys, prefix_values, span)
    other = from_partner(gone, top_bit)
    for level in range(top_bit - 1, -1, -1):
        held = join(mine, other)
        half = held.shape[0] // 2
        at = (rank >> level) & 1
        mine = lax.dynamic_slice_in_dim(held, at * half, half, 0)
        other = from_partner(lax.dynamic_slice_in_dim(held, (1 - at) * half, half, 0), level)

    members = [list(range(c, seq, 2)) for c in range(2)]
    copies = merge_part(mine, other, priv, seq // 2)
    same = lax.all_to_all(
        copies, "seq", split_axis=0, concat_axis=0, axis_index_groups=members, tiled=True
    )
    twin = from_partner(same, 0)
    columns = project(parity, same, twin, out_weight)
    pieces = columns.reshape(seq, own_rows, columns.shape[1])
    done = lax.all_to_all(pieces, "seq", split_axis=0, concat_axis=0, tiled=True)
    return done.transpose(1, 0, 2).reshape(own_rows, seq * columns.shape[1])


def solution(mesh):
    in_specs = (
        P(("groups", "seq"), None),
        P(("groups", "seq"), None),
        P(("groups", "seq"), None),
        P(("groups", "seq")),
        P(("groups", "seq"), None, None),
        P(("groups", "seq"), None, None),
        P(("groups", "seq")),
        P(("groups", "seq"), None, None),
        P(("groups", "seq"), None, None),
        P(None, "seq"),
    )
    out_specs = P(("groups", "seq"), None)
    return jax.shard_map(shards, mesh=mesh, in_specs=in_specs, out_specs=out_specs, check_vma=False)
```

```python
import functools

import jax
import jax.numpy as jnp
from jax import lax
from jax.experimental import pallas as pl
from jax.experimental.pallas import tpu as pltpu
from jax.sharding import PartitionSpec as P


HEADS = 64
KVH = 8
HD = 128
GROUP = HEADS // KVH
SCALE = HD ** (-0.5)
LOG2E = 1.4426950408889634
LANES = 128
NEG = -1e30
NT = (((1,), (1,)), ((), ()))
F32 = jnp.float32
BF16 = jnp.bfloat16


def in_hbm(array):
    return pltpu.with_memory_space_constraint(array, pltpu.HBM)


def on_chip(array):
    return pltpu.with_memory_space_constraint(array, pltpu.VMEM)


VMEM_SPEC = pl.BlockSpec(memory_space=pltpu.VMEM)
SMEM_SPEC = pl.BlockSpec(memory_space=pltpu.SMEM)


def spread_kernel(q_ref, out_ref, sems, *, blocks):
    width = out_ref.shape[2]
    moves = [
        pltpu.make_async_copy(
            q_ref.at[:, pl.ds((d // blocks) * width, width)], out_ref.at[d], sems.at[d]
        )
        for d in range(out_ref.shape[0])
    ]
    for move in moves:
        move.start()
    for move in moves:
        move.wait()


def spread(queries, seq, blocks):
    rows = queries.shape[0]
    return pl.pallas_call(
        functools.partial(spread_kernel, blocks=blocks),
        in_specs=[pl.BlockSpec(memory_space=pl.ANY)],
        out_specs=pl.BlockSpec(memory_space=pl.ANY),
        out_shape=jax.ShapeDtypeStruct((seq, rows, GROUP * HD), queries.dtype),
        scratch_shapes=[pltpu.SemaphoreType.DMA((seq,))],
        compiler_params=pltpu.CompilerParams(vmem_limit_bytes=4 << 20),
        name="spread",
    )(in_hbm(queries))


def private_kernel(par_ref, len_ref, q_ref, dk_ref, dv_ref, k_ref, v_ref, out_ref, *, draft, blocks):
    heads = GROUP // blocks
    rows = GROUP * draft
    slots = k_ref.shape[1]
    q32 = q_ref[...].astype(F32)
    query = jnp.concatenate(
        [q32[:, h * HD : (h + 1) * HD] for h in range(GROUP)], axis=0
    ).astype(BF16)
    live = lax.broadcasted_iota(jnp.int32, (rows, slots), 1) < len_ref[0]
    scores = lax.dot_general(query, k_ref[0], NT, preferred_element_type=F32) * SCALE
    scores = jnp.where(live, scores, NEG)
    seen = []
    for i in range(draft):
        bits = jnp.int32(1 << i)
        for j in range(i):
            bits = bits | jnp.where(par_ref[i] == j, seen[j], 0)
        seen.append(bits)
    row = lax.broadcasted_iota(jnp.int32, (rows, LANES), 0) % draft
    lane = lax.broadcasted_iota(jnp.int32, (rows, LANES), 1)
    shown = lane < 0
    for i in range(draft):
        for j in range(i + 1):
            hit = (seen[i] >> j) & 1
            shown = shown | ((row == i) & (lane == j) & (hit == 1))
    fill = jnp.zeros((LANES - draft, HD), F32)
    dkey = jnp.concatenate([dk_ref[...].astype(F32), fill], axis=0).astype(BF16)
    dval = jnp.concatenate([dv_ref[...].astype(F32), fill], axis=0).astype(BF16)
    tree = lax.dot_general(query, dkey, NT, preferred_element_type=F32) * SCALE
    tree = jnp.where(shown, tree, NEG)
    peak = jnp.maximum(
        jnp.max(scores, axis=1, keepdims=True), jnp.max(tree, axis=1, keepdims=True)
    )
    weights = jnp.exp(scores - peak)
    tree_w = jnp.exp(tree - peak)
    denom = jnp.sum(weights, axis=1, keepdims=True) + jnp.sum(tree_w, axis=1, keepdims=True)
    mixture = jnp.dot(weights.astype(BF16), v_ref[0], preferred_element_type=F32)
    mixture = mixture + jnp.dot(tree_w.astype(BF16), dval, preferred_element_type=F32)
    mixture = mixture / denom
    lse = peak + jnp.log(denom)
    stat_lane = lax.broadcasted_iota(jnp.int32, (draft, LANES), 1)
    for b in range(blocks):
        stats = jnp.zeros((draft, LANES), F32)
        for hh in range(heads):
            lo = (b * heads + hh) * draft
            out_ref[b, :, hh * HD : (hh + 1) * HD] = mixture[lo : lo + draft]
            stats = jnp.where(stat_lane == hh, lse[lo : lo + draft], stats)
        out_ref[b, :, heads * HD :] = stats


def private_part(parents, lengths, queries, dkeys, dvals, pkeys, pvals, blocks):
    draft = queries.shape[0]
    slots = pkeys.shape[1]
    wide = (GROUP // blocks) * HD + LANES
    smem = pl.BlockSpec(memory_space=pltpu.SMEM)
    return pl.pallas_call(
        functools.partial(private_kernel, draft=draft, blocks=blocks),
        grid=(KVH,),
        in_specs=[
            smem,
            smem,
            pl.BlockSpec((draft, GROUP * HD), lambda g: (0, g)),
            pl.BlockSpec((draft, HD), lambda g: (0, g)),
            pl.BlockSpec((draft, HD), lambda g: (0, g)),
            pl.BlockSpec((1, slots, HD), lambda g: (0, 0, g)),
            pl.BlockSpec((1, slots, HD), lambda g: (0, 0, g)),
        ],
        out_specs=pl.BlockSpec((blocks, draft, wide), lambda g: (g, 0, 0)),
        out_shape=jax.ShapeDtypeStruct((KVH * blocks, draft, wide), F32),
        cost_estimate=pl.CostEstimate(
            flops=4 * draft * HEADS * slots * HD,
            transcendentals=draft * HEADS * slots,
            bytes_accessed=4 * slots * KVH * HD,
        ),
        name="private_part",
    )(parents, lengths, queries, dkeys, dvals, pkeys, pvals)


def prefix_kernel(
    rank_ref, q_ref, k_ref, v_ref, keep_ref, send_ref, q32, qs, peak, denom, acc, *, sub
):
    step = pl.program_id(0)
    owners, draft, _ = q_ref.shape
    rows = owners * draft

    @pl.when(step == 0)
    def _():
        for s in range(owners):
            q32[s * draft : (s + 1) * draft, :] = q_ref[s].astype(F32)
        for h in range(GROUP):
            qs[h * rows : (h + 1) * rows, :] = q32[:, h * HD : (h + 1) * HD].astype(BF16)
        peak[...] = jnp.full(peak.shape, NEG, F32)
        denom[...] = jnp.zeros(denom.shape, F32)
        acc[...] = jnp.zeros(acc.shape, F32)

    span = k_ref.shape[1]
    count = span // sub

    def score(b):
        block = k_ref[0, b * sub : (b + 1) * sub, :]
        return lax.dot_general(qs[...], block, NT, preferred_element_type=F32)

    top, total, mixed = peak[...], denom[...], acc[...]
    scores = score(0)
    for b in range(count):
        ahead = score(b + 1) if b + 1 < count else None
        tiles = [scores[:, j : j + LANES] for j in range(0, sub, LANES)]
        block_top = functools.reduce(jnp.maximum, tiles)
        new = jnp.maximum(top, jnp.max(block_top, axis=1, keepdims=True) * (SCALE * LOG2E))
        fade = jnp.exp2(top - new)
        parts = [jnp.exp2(tile * (SCALE * LOG2E) - new) for tile in tiles]
        total = total * fade + functools.reduce(jnp.add, parts)
        weights = jnp.concatenate([part.astype(BF16) for part in parts], axis=1)
        block = v_ref[0, b * sub : (b + 1) * sub, :]
        mixed = mixed * fade + jnp.dot(weights, block, preferred_element_type=F32)
        top, scores = new, ahead
    peak[...], denom[...], acc[...] = top, total, mixed

    @pl.when(step == pl.num_programs(0) - 1)
    def _():
        total = jnp.sum(denom[...], axis=1, keepdims=True)
        acc[...] = acc[...] / total
        denom[...] = peak[...] * (1.0 / LOG2E) + jnp.log(total)
        half = keep_ref.shape[0]
        mine = pl.multiple_of(rank_ref[0] * half, half)
        other = pl.multiple_of((1 - rank_ref[0]) * half, half)
        keep_ref[:, :HD] = acc[pl.ds(mine, half), :]
        keep_ref[:, HD:] = denom[pl.ds(mine, half), :]
        send_ref[:, :HD] = acc[pl.ds(other, half), :]
        send_ref[:, HD:] = denom[pl.ds(other, half), :]


def prefix_part(side, queries, keys, values, span, sub):
    owners, draft, _ = queries.shape
    rows = owners * draft * GROUP
    shape = jax.ShapeDtypeStruct((rows // 2, HD + LANES), F32)
    return pl.pallas_call(
        functools.partial(prefix_kernel, sub=sub),
        grid_spec=pltpu.PrefetchScalarGridSpec(
            num_scalar_prefetch=1,
            grid=(keys.shape[1] // span,),
            in_specs=[
                pl.BlockSpec(queries.shape, lambda i, r: (0, 0, 0)),
                pl.BlockSpec((1, span, HD), lambda i, r: (0, i, 0)),
                pl.BlockSpec((1, span, HD), lambda i, r: (0, i, 0)),
            ],
            out_specs=[
                pl.BlockSpec((rows // 2, HD + LANES), lambda i, r: (0, 0)),
                pl.BlockSpec((rows // 2, HD + LANES), lambda i, r: (0, 0)),
            ],
            scratch_shapes=[
                pltpu.VMEM((owners * draft, GROUP * HD), F32),
                pltpu.VMEM((rows, HD), BF16),
                pltpu.VMEM((rows, LANES), F32),
                pltpu.VMEM((rows, LANES), F32),
                pltpu.VMEM((rows, HD), F32),
            ],
        ),
        out_shape=[shape, shape],
        compiler_params=pltpu.CompilerParams(vmem_limit_bytes=32 << 20),
        cost_estimate=pl.CostEstimate(
            flops=4 * rows * keys.shape[1] * HD,
            transcendentals=rows * keys.shape[1],
            bytes_accessed=4 * keys.shape[1] * HD,
        ),
        name="prefix_part",
    )(side, queries, in_hbm(keys), in_hbm(values))


def join(first, second):
    out_a, lse_a = first[:, :HD], first[:, HD:]
    out_b, lse_b = second[:, :HD], second[:, HD:]
    top = jnp.maximum(lse_a, lse_b)
    scale_a = jnp.exp(lse_a - top)
    scale_b = jnp.exp(lse_b - top)
    both = scale_a + scale_b
    return jnp.concatenate(
        [(scale_a * out_a + scale_b * out_b) / both, top + jnp.log(both)], axis=1
    )


def merge_kernel(side_ref, mine_ref, other_ref, priv_ref, w_ref, att_ref, wide_ref, p32, sem):
    fetch = pltpu.make_async_copy(w_ref.at[:, side_ref[0]], wide_ref, sem)
    fetch.start()
    owners, draft, wide = priv_ref.shape
    rows = owners * draft
    heads = (wide - LANES) // HD
    for s in range(owners):
        p32[s * draft : (s + 1) * draft, :] = priv_ref[s]
    for h in range(heads):
        part = slice(h * rows, (h + 1) * rows)
        lse_p = p32[:, heads * HD + h : heads * HD + h + 1]
        lse_a = mine_ref[part, HD:]
        lse_b = other_ref[part, HD:]
        top = jnp.maximum(jnp.maximum(lse_a, lse_b), lse_p)
        scale_a = jnp.exp(lse_a - top)
        scale_b = jnp.exp(lse_b - top)
        scale_p = jnp.exp(lse_p - top)
        mixed = (
            scale_a * mine_ref[part, :HD]
            + scale_b * other_ref[part, :HD]
            + scale_p * p32[:, h * HD : (h + 1) * HD]
        ) / (scale_a + scale_b + scale_p)
        mixed = mixed.astype(BF16)
        for copy in range(att_ref.shape[0]):
            att_ref[copy, :, h * HD : (h + 1) * HD] = mixed
    fetch.wait()


def merge_part(side, mine, other, priv, weight):
    owners, draft, wide = priv.shape
    chips, _, deep, cols = weight.shape
    return pl.pallas_call(
        merge_kernel,
        in_specs=[SMEM_SPEC, VMEM_SPEC, VMEM_SPEC, VMEM_SPEC, pl.BlockSpec(memory_space=pl.ANY)],
        out_specs=[VMEM_SPEC, VMEM_SPEC],
        out_shape=[
            pltpu.VMEM((chips, owners * draft, wide - LANES), BF16),
            pltpu.VMEM((chips, deep, cols), BF16),
        ],
        scratch_shapes=[pltpu.VMEM((owners * draft, wide), F32), pltpu.SemaphoreType.DMA],
        compiler_params=pltpu.CompilerParams(vmem_limit_bytes=8 << 20),
        cost_estimate=pl.CostEstimate(
            flops=8 * mine.size, transcendentals=mine.size, bytes_accessed=2 * chips * deep * cols
        ),
        name="merge_part",
    )(side, on_chip(mine), on_chip(other), on_chip(priv), in_hbm(weight))


def matmuls(att_ref, wide_ref):
    return functools.reduce(
        jnp.add,
        [
            jnp.dot(att_ref[i], wide_ref[i], preferred_element_type=F32)
            for i in range(att_ref.shape[0])
        ],
    )


def first_kernel(side_ref, att_ref, wide_ref, w_ref, out_ref, next_ref, sem):
    fetch = pltpu.make_async_copy(w_ref.at[:, 1 - side_ref[0]], next_ref, sem)
    fetch.start()
    out_ref[...] = matmuls(att_ref, wide_ref)
    fetch.wait()


def second_kernel(part_ref, att_ref, wide_ref, out_ref):
    total = part_ref[...] + matmuls(att_ref, wide_ref)
    owners, draft, _ = out_ref.shape
    for s in range(owners):
        out_ref[s] = total[s * draft : (s + 1) * draft].astype(BF16)


def project_own(side, att, wide, weight):
    chips, rows, deep = att.shape
    cols = weight.shape[3]
    return pl.pallas_call(
        first_kernel,
        in_specs=[SMEM_SPEC, VMEM_SPEC, VMEM_SPEC, pl.BlockSpec(memory_space=pl.ANY)],
        out_specs=[VMEM_SPEC, VMEM_SPEC],
        out_shape=[pltpu.VMEM((rows, cols), F32), pltpu.VMEM((chips, deep, cols), BF16)],
        scratch_shapes=[pltpu.SemaphoreType.DMA],
        compiler_params=pltpu.CompilerParams(vmem_limit_bytes=8 << 20),
        cost_estimate=pl.CostEstimate(
            flops=2 * rows * deep * chips * cols,
            transcendentals=0,
            bytes_accessed=2 * deep * chips * cols,
        ),
        name="project_own",
    )(side, on_chip(att), on_chip(wide), in_hbm(weight))


def project_twin(part, att, wide, owners):
    chips, rows, deep = att.shape
    cols = wide.shape[2]
    return pl.pallas_call(
        second_kernel,
        in_specs=[VMEM_SPEC, VMEM_SPEC, VMEM_SPEC],
        out_specs=VMEM_SPEC,
        out_shape=pltpu.VMEM((owners, rows // owners, cols), BF16),
        compiler_params=pltpu.CompilerParams(vmem_limit_bytes=8 << 20),
        cost_estimate=pl.CostEstimate(
            flops=2 * rows * deep * chips * cols, transcendentals=0, bytes_accessed=0
        ),
        name="project_twin",
    )(on_chip(part), on_chip(att), on_chip(wide))


def shards(
    queries,
    draft_keys,
    draft_values,
    parents,
    private_keys,
    private_values,
    priv_lengths,
    prefix_keys,
    prefix_values,
    out_weight,
):
    own_rows = queries.shape[0]
    seq = lax.axis_size("seq")
    blocks = seq // KVH
    device = lax.axis_index("seq")
    rank = device % blocks
    top_bit = blocks.bit_length() - 2
    side = ((rank >> top_bit) & 1).astype(jnp.int32).reshape(1)
    parity = (device % 2).astype(jnp.int32).reshape(1)

    def from_partner(array, bit):
        return lax.ppermute(array, "seq", [(i, i ^ 1 << bit) for i in range(seq)])

    ask = spread(queries, seq, blocks)
    every_query = lax.all_to_all(ask, "seq", split_axis=0, concat_axis=0, tiled=True)

    told = private_part(
        parents, priv_lengths, queries, draft_keys, draft_values, private_keys, private_values, blocks
    )
    priv = lax.all_to_all(told, "seq", split_axis=0, concat_axis=0, tiled=True)

    span = min(4096, prefix_keys.shape[1])
    mine, gone = prefix_part(
        side, every_query, prefix_keys, prefix_values, span, span // 4
    )
    other = from_partner(gone, top_bit)
    for level in range(top_bit - 1, -1, -1):
        held = join(mine, other)
        half = held.shape[0] // 2
        at = (rank >> level) & 1
        mine = lax.dynamic_slice_in_dim(held, at * half, half, 0)
        other = from_partner(lax.dynamic_slice_in_dim(held, (1 - at) * half, half, 0), level)

    members = [list(range(c, seq, 2)) for c in range(2)]
    weight = out_weight.reshape(seq // 2, 2, -1, out_weight.shape[1])
    copies, wide = merge_part(parity, mine, other, priv, weight)
    same = lax.all_to_all(
        copies, "seq", split_axis=0, concat_axis=0, axis_index_groups=members, tiled=True
    )
    twin = from_partner(same, 0)
    part, wide = project_own(parity, same, wide, weight)
    pieces = project_twin(part, twin, wide, seq)
    done = lax.all_to_all(pieces, "seq", split_axis=0, concat_axis=0, tiled=True)
    return done.transpose(1, 0, 2).reshape(own_rows, -1).astype(F32)


def solution(mesh):
    in_specs = (
        P(("groups", "seq"), None),
        P(("groups", "seq"), None),
        P(("groups", "seq"), None),
        P(("groups", "seq")),
        P(("groups", "seq"), None, None),
        P(("groups", "seq"), None, None),
        P(("groups", "seq")),
        P(("groups", "seq"), None, None),
        P(("groups", "seq"), None, None),
        P(None, "seq"),
    )
    out_specs = P(("groups", "seq"), None)

    return jax.shard_map(shards, mesh=mesh, in_specs=in_specs, out_specs=out_specs, check_vma=False)
```

```python
import functools

import jax
import jax.numpy as jnp
from jax import lax
from jax.experimental import pallas as pl
from jax.experimental.pallas import tpu as pltpu
from jax.sharding import PartitionSpec as P


HEADS = 64
KVH = 8
HD = 128
GROUP = HEADS // KVH
SCALE = HD ** (-0.5)
LOG2E = 1.4426950408889634
LANES = 128
NEG = -1e30
NT = (((1,), (1,)), ((), ()))
F32 = jnp.float32
BF16 = jnp.bfloat16


def in_hbm(array):
    return pltpu.with_memory_space_constraint(array, pltpu.HBM)


def on_chip(array):
    return pltpu.with_memory_space_constraint(array, pltpu.VMEM)


VMEM_SPEC = pl.BlockSpec(memory_space=pltpu.VMEM)
SMEM_SPEC = pl.BlockSpec(memory_space=pltpu.SMEM)


def private_kernel(
    par_ref, len_ref, q_ref, dk_ref, dv_ref, k_ref, v_ref, out_ref, ask_ref, *, draft, blocks, batch
):
    heads = GROUP // blocks
    rows = GROUP * draft
    slots = k_ref.shape[1]
    seen = []
    for i in range(draft):
        bits = jnp.int32(1 << i)
        for j in range(i):
            bits = bits | jnp.where(par_ref[i] == j, seen[j], 0)
        seen.append(bits)
    row = lax.broadcasted_iota(jnp.int32, (rows, LANES), 0) % draft
    lane = lax.broadcasted_iota(jnp.int32, (rows, LANES), 1)
    mask = jnp.zeros((rows, LANES), jnp.int32)
    for i in range(draft):
        mask = jnp.where(row == i, seen[i], mask)
    shown = (lane < draft) & ((lax.shift_right_logical(mask, jnp.minimum(lane, 31)) & 1) == 1)
    live = lax.broadcasted_iota(jnp.int32, (rows, slots), 1) < len_ref[0]
    fill = jnp.zeros((LANES - draft, HD), F32)
    stat_lane = lax.broadcasted_iota(jnp.int32, (draft, LANES), 1)
    groups = range(batch)
    wide = GROUP * HD
    queries = []
    for g in groups:
        q = q_ref[:, g * wide : (g + 1) * wide]
        for b in range(blocks):
            ask_ref[g * blocks + b] = q
        q32 = q.astype(F32)
        queries.append(
            jnp.concatenate([q32[:, h * HD : (h + 1) * HD] for h in range(GROUP)], axis=0).astype(BF16)
        )
    cols = [slice(g * HD, (g + 1) * HD) for g in groups]
    scores = [
        lax.dot_general(queries[g], k_ref[0, :, cols[g]], NT, preferred_element_type=F32) for g in groups
    ]
    trees = []
    for g in groups:
        dkey = jnp.concatenate([dk_ref[:, cols[g]].astype(F32), fill], axis=0).astype(BF16)
        trees.append(lax.dot_general(queries[g], dkey, NT, preferred_element_type=F32))
    for g in groups:
        score = jnp.where(live, scores[g] * SCALE, NEG)
        tree = jnp.where(shown, trees[g] * SCALE, NEG)
        tiles = [score[:, j : j + LANES] for j in range(0, slots, LANES)] + [tree]
        peak = jnp.max(functools.reduce(jnp.maximum, tiles), axis=1, keepdims=True)
        tiles = [jnp.exp(tile - peak) for tile in tiles]
        denom = jnp.sum(functools.reduce(jnp.add, tiles), axis=1, keepdims=True)
        weights = jnp.concatenate([tile.astype(BF16) for tile in tiles[:-1]], axis=1)
        dval = jnp.concatenate([dv_ref[:, cols[g]].astype(F32), fill], axis=0).astype(BF16)
        mixture = jnp.dot(weights, v_ref[0, :, cols[g]], preferred_element_type=F32)
        mixture = mixture + jnp.dot(tiles[-1].astype(BF16), dval, preferred_element_type=F32)
        mixture = mixture / denom
        lse = peak + jnp.log(denom)
        for b in range(blocks):
            stats = jnp.zeros((draft, LANES), F32)
            for hh in range(heads):
                lo = (b * heads + hh) * draft
                out_ref[g * blocks + b, :, hh * HD : (hh + 1) * HD] = mixture[lo : lo + draft]
                stats = jnp.where(stat_lane == hh, lse[lo : lo + draft], stats)
            out_ref[g * blocks + b, :, heads * HD :] = stats


def private_part(parents, lengths, queries, dkeys, dvals, pkeys, pvals, blocks, batch):
    draft = queries.shape[0]
    slots = pkeys.shape[1]
    wide = (GROUP // blocks) * HD + LANES
    return pl.pallas_call(
        functools.partial(private_kernel, draft=draft, blocks=blocks, batch=batch),
        grid=(KVH // batch,),
        in_specs=[
            SMEM_SPEC,
            SMEM_SPEC,
            pl.BlockSpec((draft, batch * GROUP * HD), lambda g: (0, g)),
            pl.BlockSpec((draft, batch * HD), lambda g: (0, g)),
            pl.BlockSpec((draft, batch * HD), lambda g: (0, g)),
            pl.BlockSpec((1, slots, batch * HD), lambda g: (0, 0, g)),
            pl.BlockSpec((1, slots, batch * HD), lambda g: (0, 0, g)),
        ],
        out_specs=[
            pl.BlockSpec((batch * blocks, draft, wide), lambda g: (g, 0, 0)),
            pl.BlockSpec((batch * blocks, draft, GROUP * HD), lambda g: (g, 0, 0)),
        ],
        out_shape=[
            jax.ShapeDtypeStruct((KVH * blocks, draft, wide), F32),
            jax.ShapeDtypeStruct((KVH * blocks, draft, GROUP * HD), BF16),
        ],
        cost_estimate=pl.CostEstimate(
            flops=4 * draft * HEADS * slots * HD,
            transcendentals=draft * HEADS * slots,
            bytes_accessed=4 * slots * KVH * HD,
        ),
        name="private_part",
    )(parents, lengths, queries, dkeys, dvals, pkeys, pvals)


def prefix_kernel(
    rank_ref, q_ref, k_ref, v_ref, keep_ref, send_ref, q32, qs, peak, denom, acc, *, sub
):
    step = pl.program_id(0)
    owners, draft, _ = q_ref.shape
    rows = owners * draft

    @pl.when(step == 0)
    def _():
        for s in range(owners):
            q32[s * draft : (s + 1) * draft, :] = q_ref[s].astype(F32)
        for h in range(GROUP):
            qs[h * rows : (h + 1) * rows, :] = q32[:, h * HD : (h + 1) * HD].astype(BF16)
        peak[...] = jnp.full(peak.shape, NEG, F32)
        denom[...] = jnp.zeros(denom.shape, F32)
        acc[...] = jnp.zeros(acc.shape, F32)

    span = k_ref.shape[1]
    count = span // sub

    def score(b):
        block = k_ref[0, b * sub : (b + 1) * sub, :]
        return lax.dot_general(qs[...], block, NT, preferred_element_type=F32)

    top, total, mixed = peak[...], denom[...], acc[...]
    scores = score(0)
    for b in range(count):
        ahead = score(b + 1) if b + 1 < count else None
        tiles = [scores[:, j : j + LANES] for j in range(0, sub, LANES)]
        block_top = functools.reduce(jnp.maximum, tiles)
        new = jnp.maximum(top, jnp.max(block_top, axis=1, keepdims=True) * (SCALE * LOG2E))
        fade = jnp.exp2(top - new)
        parts = [jnp.exp2(tile * (SCALE * LOG2E) - new) for tile in tiles]
        total = total * fade + functools.reduce(jnp.add, parts)
        weights = jnp.concatenate([part.astype(BF16) for part in parts], axis=1)
        block = v_ref[0, b * sub : (b + 1) * sub, :]
        mixed = mixed * fade + jnp.dot(weights, block, preferred_element_type=F32)
        top, scores = new, ahead
    peak[...], denom[...], acc[...] = top, total, mixed

    @pl.when(step == pl.num_programs(0) - 1)
    def _():
        total = jnp.sum(denom[...], axis=1, keepdims=True)
        acc[...] = acc[...] / total
        denom[...] = peak[...] * (1.0 / LOG2E) + jnp.log(total)
        half = keep_ref.shape[0]
        mine = pl.multiple_of(rank_ref[0] * half, half)
        other = pl.multiple_of((1 - rank_ref[0]) * half, half)
        keep_ref[:, :HD] = acc[pl.ds(mine, half), :]
        keep_ref[:, HD:] = denom[pl.ds(mine, half), :]
        send_ref[:, :HD] = acc[pl.ds(other, half), :]
        send_ref[:, HD:] = denom[pl.ds(other, half), :]


def prefix_part(side, queries, keys, values, span, sub):
    owners, draft, _ = queries.shape
    rows = owners * draft * GROUP
    shape = jax.ShapeDtypeStruct((rows // 2, HD + LANES), F32)
    return pl.pallas_call(
        functools.partial(prefix_kernel, sub=sub),
        grid_spec=pltpu.PrefetchScalarGridSpec(
            num_scalar_prefetch=1,
            grid=(keys.shape[1] // span,),
            in_specs=[
                pl.BlockSpec(queries.shape, lambda i, r: (0, 0, 0)),
                pl.BlockSpec((1, span, HD), lambda i, r: (0, i, 0)),
                pl.BlockSpec((1, span, HD), lambda i, r: (0, i, 0)),
            ],
            out_specs=[
                pl.BlockSpec((rows // 2, HD + LANES), lambda i, r: (0, 0)),
                pl.BlockSpec((rows // 2, HD + LANES), lambda i, r: (0, 0)),
            ],
            scratch_shapes=[
                pltpu.VMEM((owners * draft, GROUP * HD), F32),
                pltpu.VMEM((rows, HD), BF16),
                pltpu.VMEM((rows, LANES), F32),
                pltpu.VMEM((rows, LANES), F32),
                pltpu.VMEM((rows, HD), F32),
            ],
        ),
        out_shape=[shape, shape],
        compiler_params=pltpu.CompilerParams(vmem_limit_bytes=32 << 20),
        cost_estimate=pl.CostEstimate(
            flops=4 * rows * keys.shape[1] * HD,
            transcendentals=rows * keys.shape[1],
            bytes_accessed=4 * keys.shape[1] * HD,
        ),
        name="prefix_part",
    )(side, queries, in_hbm(keys), in_hbm(values))


def join(first, second):
    out_a, lse_a = first[:, :HD], first[:, HD:]
    out_b, lse_b = second[:, :HD], second[:, HD:]
    top = jnp.maximum(lse_a, lse_b)
    scale_a = jnp.exp(lse_a - top)
    scale_b = jnp.exp(lse_b - top)
    both = scale_a + scale_b
    return jnp.concatenate(
        [(scale_a * out_a + scale_b * out_b) / both, top + jnp.log(both)], axis=1
    )


def merge_kernel(side_ref, mine_ref, other_ref, priv_ref, w_ref, att_ref, wide_ref, p32, sem):
    fetch = pltpu.make_async_copy(w_ref.at[:, side_ref[0]], wide_ref, sem)
    fetch.start()
    owners, draft, wide = priv_ref.shape
    rows = owners * draft
    heads = (wide - LANES) // HD
    for s in range(owners):
        p32[s * draft : (s + 1) * draft, :] = priv_ref[s]
    for h in range(heads):
        part = slice(h * rows, (h + 1) * rows)
        lse_p = p32[:, heads * HD + h : heads * HD + h + 1]
        lse_a = mine_ref[part, HD:]
        lse_b = other_ref[part, HD:]
        top = jnp.maximum(jnp.maximum(lse_a, lse_b), lse_p)
        scale_a = jnp.exp(lse_a - top)
        scale_b = jnp.exp(lse_b - top)
        scale_p = jnp.exp(lse_p - top)
        mixed = (
            scale_a * mine_ref[part, :HD]
            + scale_b * other_ref[part, :HD]
            + scale_p * p32[:, h * HD : (h + 1) * HD]
        ) / (scale_a + scale_b + scale_p)
        mixed = mixed.astype(BF16)
        for copy in range(att_ref.shape[0]):
            att_ref[copy, :, h * HD : (h + 1) * HD] = mixed
    fetch.wait()


def merge_part(side, mine, other, priv, weight):
    owners, draft, wide = priv.shape
    chips, _, deep, cols = weight.shape
    return pl.pallas_call(
        merge_kernel,
        in_specs=[SMEM_SPEC, VMEM_SPEC, VMEM_SPEC, VMEM_SPEC, pl.BlockSpec(memory_space=pl.ANY)],
        out_specs=[VMEM_SPEC, VMEM_SPEC],
        out_shape=[
            pltpu.VMEM((chips, owners * draft, wide - LANES), BF16),
            pltpu.VMEM((chips, deep, cols), BF16),
        ],
        scratch_shapes=[pltpu.VMEM((owners * draft, wide), F32), pltpu.SemaphoreType.DMA],
        compiler_params=pltpu.CompilerParams(vmem_limit_bytes=8 << 20),
        cost_estimate=pl.CostEstimate(
            flops=8 * mine.size, transcendentals=mine.size, bytes_accessed=2 * chips * deep * cols
        ),
        name="merge_part",
    )(side, on_chip(mine), on_chip(other), on_chip(priv), in_hbm(weight))


def matmuls(att_ref, wide_ref):
    return functools.reduce(
        jnp.add,
        [
            jnp.dot(att_ref[i], wide_ref[i], preferred_element_type=F32)
            for i in range(att_ref.shape[0])
        ],
    )


def first_kernel(side_ref, att_ref, wide_ref, w_ref, out_ref, next_ref, sem):
    fetch = pltpu.make_async_copy(w_ref.at[:, 1 - side_ref[0]], next_ref, sem)
    fetch.start()
    out_ref[...] = matmuls(att_ref, wide_ref)
    fetch.wait()


def second_kernel(part_ref, att_ref, wide_ref, out_ref):
    total = part_ref[...] + matmuls(att_ref, wide_ref)
    owners, draft, _ = out_ref.shape
    for s in range(owners):
        out_ref[s] = total[s * draft : (s + 1) * draft].astype(BF16)


def project_own(side, att, wide, weight):
    chips, rows, deep = att.shape
    cols = weight.shape[3]
    return pl.pallas_call(
        first_kernel,
        in_specs=[SMEM_SPEC, VMEM_SPEC, VMEM_SPEC, pl.BlockSpec(memory_space=pl.ANY)],
        out_specs=[VMEM_SPEC, VMEM_SPEC],
        out_shape=[pltpu.VMEM((rows, cols), F32), pltpu.VMEM((chips, deep, cols), BF16)],
        scratch_shapes=[pltpu.SemaphoreType.DMA],
        compiler_params=pltpu.CompilerParams(vmem_limit_bytes=8 << 20),
        cost_estimate=pl.CostEstimate(
            flops=2 * rows * deep * chips * cols,
            transcendentals=0,
            bytes_accessed=2 * deep * chips * cols,
        ),
        name="project_own",
    )(side, on_chip(att), on_chip(wide), in_hbm(weight))


def project_twin(part, att, wide, owners):
    chips, rows, deep = att.shape
    cols = wide.shape[2]
    return pl.pallas_call(
        second_kernel,
        in_specs=[VMEM_SPEC, VMEM_SPEC, VMEM_SPEC],
        out_specs=VMEM_SPEC,
        out_shape=pltpu.VMEM((owners, rows // owners, cols), BF16),
        compiler_params=pltpu.CompilerParams(vmem_limit_bytes=8 << 20),
        cost_estimate=pl.CostEstimate(
            flops=2 * rows * deep * chips * cols, transcendentals=0, bytes_accessed=0
        ),
        name="project_twin",
    )(on_chip(part), on_chip(att), on_chip(wide))


def shards(
    queries,
    draft_keys,
    draft_values,
    parents,
    private_keys,
    private_values,
    priv_lengths,
    prefix_keys,
    prefix_values,
    out_weight,
):
    own_rows = queries.shape[0]
    seq = lax.axis_size("seq")
    blocks = seq // KVH
    device = lax.axis_index("seq")
    rank = device % blocks
    top_bit = blocks.bit_length() - 2
    side = ((rank >> top_bit) & 1).astype(jnp.int32).reshape(1)
    parity = (device % 2).astype(jnp.int32).reshape(1)

    def from_partner(array, bit):
        return lax.ppermute(array, "seq", [(i, i ^ 1 << bit) for i in range(seq)])

    told, ask = private_part(
        parents,
        priv_lengths,
        queries,
        draft_keys,
        draft_values,
        in_hbm(private_keys),
        in_hbm(private_values),
        blocks,
        KVH // 2,
    )
    every_query = lax.all_to_all(ask, "seq", split_axis=0, concat_axis=0, tiled=True)
    priv = lax.all_to_all(told, "seq", split_axis=0, concat_axis=0, tiled=True)

    span = min(4096, prefix_keys.shape[1])
    mine, gone = prefix_part(
        side, every_query, prefix_keys, prefix_values, span, span // 4
    )
    other = from_partner(gone, top_bit)
    for level in range(top_bit - 1, -1, -1):
        held = join(mine, other)
        half = held.shape[0] // 2
        at = (rank >> level) & 1
        mine = lax.dynamic_slice_in_dim(held, at * half, half, 0)
        other = from_partner(lax.dynamic_slice_in_dim(held, (1 - at) * half, half, 0), level)

    members = [list(range(c, seq, 2)) for c in range(2)]
    weight = out_weight.reshape(seq // 2, 2, -1, out_weight.shape[1])
    copies, wide = merge_part(parity, mine, other, priv, weight)
    same = lax.all_to_all(
        copies, "seq", split_axis=0, concat_axis=0, axis_index_groups=members, tiled=True
    )
    twin = from_partner(same, 0)
    part, wide = project_own(parity, same, wide, weight)
    pieces = project_twin(part, twin, wide, seq)
    done = lax.all_to_all(pieces, "seq", split_axis=0, concat_axis=0, tiled=True)
    return done.transpose(1, 0, 2).reshape(own_rows, -1).astype(F32)


def solution(mesh):
    in_specs = (
        P(("groups", "seq"), None),
        P(("groups", "seq"), None),
        P(("groups", "seq"), None),
        P(("groups", "seq")),
        P(("groups", "seq"), None, None),
        P(("groups", "seq"), None, None),
        P(("groups", "seq")),
        P(("groups", "seq"), None, None),
        P(("groups", "seq"), None, None),
        P(None, "seq"),
    )
    out_specs = P(("groups", "seq"), None)

    return jax.shard_map(shards, mesh=mesh, in_specs=in_specs, out_specs=out_specs, check_vma=False)
```

```python
import functools

import jax
import jax.numpy as jnp
from jax import lax
from jax.experimental import pallas as pl
from jax.experimental.pallas import tpu as pltpu
from jax.sharding import PartitionSpec as P


HEADS = 64
KVH = 8
HD = 128
GROUP = HEADS // KVH
SCALE = HD ** (-0.5)
LOG2E = 1.4426950408889634
LANES = 128
NEG = -1e30
LIMIT = 2.0**100
WIDE = GROUP * HD
MESSAGE = 3 * WIDE + LANES
NT = (((1,), (1,)), ((), ()))
TN = (((0,), (0,)), ((), ()))
F32 = jnp.float32
BF16 = jnp.bfloat16


def in_hbm(array):
    return pltpu.with_memory_space_constraint(array, pltpu.HBM)


def on_chip(array):
    return pltpu.with_memory_space_constraint(array, pltpu.VMEM)


VMEM_SPEC = pl.BlockSpec(memory_space=pltpu.VMEM)
SMEM_SPEC = pl.BlockSpec(memory_space=pltpu.SMEM)


def private_kernel(
    par_ref, len_ref, q_ref, dk_ref, dv_ref, k_ref, v_ref, out_ref, *, draft, copies, batch
):
    rows = GROUP * draft
    slots = k_ref.shape[1]
    seen = []
    for i in range(draft):
        bits = jnp.int32(1 << i)
        for j in range(i):
            bits = bits | jnp.where(par_ref[i] == j, seen[j], 0)
        seen.append(bits)
    row = lax.broadcasted_iota(jnp.int32, (rows, LANES), 0) % draft
    lane = lax.broadcasted_iota(jnp.int32, (rows, LANES), 1)
    mask = jnp.zeros((rows, LANES), jnp.int32)
    for i in range(draft):
        mask = jnp.where(row == i, seen[i], mask)
    shown = (lane < draft) & ((lax.shift_right_logical(mask, jnp.minimum(lane, 31)) & 1) == 1)
    live = lax.broadcasted_iota(jnp.int32, (rows, slots), 1) < len_ref[0]
    fill = jnp.zeros((LANES - draft, HD), F32)
    stat_lane = lax.broadcasted_iota(jnp.int32, (draft, LANES), 1)
    groups = range(batch)
    queries = []
    for g in groups:
        q = q_ref[:, g * WIDE : (g + 1) * WIDE]
        for copy in range(copies):
            out_ref[g * copies + copy, :, :WIDE] = q
        q32 = q.astype(F32)
        queries.append(
            jnp.concatenate([q32[:, h * HD : (h + 1) * HD] for h in range(GROUP)], axis=0).astype(BF16)
        )
    cols = [slice(g * HD, (g + 1) * HD) for g in groups]
    scores = [
        lax.dot_general(queries[g], k_ref[0, :, cols[g]], NT, preferred_element_type=F32) for g in groups
    ]
    trees = []
    for g in groups:
        dkey = jnp.concatenate([dk_ref[:, cols[g]].astype(F32), fill], axis=0).astype(BF16)
        trees.append(lax.dot_general(queries[g], dkey, NT, preferred_element_type=F32))
    for g in groups:
        score = jnp.where(live, scores[g] * SCALE, NEG)
        tree = jnp.where(shown, trees[g] * SCALE, NEG)
        tiles = [score[:, j : j + LANES] for j in range(0, slots, LANES)] + [tree]
        peak = jnp.max(functools.reduce(jnp.maximum, tiles), axis=1, keepdims=True)
        tiles = [jnp.exp(tile - peak) for tile in tiles]
        denom = jnp.sum(functools.reduce(jnp.add, tiles), axis=1, keepdims=True)
        weights = jnp.concatenate([tile.astype(BF16) for tile in tiles[:-1]], axis=1)
        dval = jnp.concatenate([dv_ref[:, cols[g]].astype(F32), fill], axis=0).astype(BF16)
        mixture = jnp.dot(weights, v_ref[0, :, cols[g]], preferred_element_type=F32)
        mixture = mixture + jnp.dot(tiles[-1].astype(BF16), dval, preferred_element_type=F32)
        mixture = mixture / denom
        coarse = mixture.astype(BF16).astype(F32)
        fine = mixture - coarse
        lse = peak + jnp.log(denom)
        first = lse.astype(BF16).astype(F32)
        second = (lse - first).astype(BF16).astype(F32)
        third = lse - first - second
        stats = jnp.zeros((draft, LANES), F32)
        for copy in range(copies):
            at = g * copies + copy
            for h in range(GROUP):
                part = slice(h * draft, (h + 1) * draft)
                out_ref[at, :, WIDE + h * HD : WIDE + (h + 1) * HD] = coarse[part].astype(BF16)
                out_ref[at, :, 2 * WIDE + h * HD : 2 * WIDE + (h + 1) * HD] = fine[part].astype(BF16)
                if copy == 0:
                    for t, term in enumerate((first, second, third)):
                        stats = jnp.where(stat_lane == 3 * h + t, term[part], stats)
            out_ref[at, :, 3 * WIDE :] = stats.astype(BF16)


def private_part(parents, lengths, queries, dkeys, dvals, pkeys, pvals, copies, batch):
    draft = queries.shape[0]
    slots = pkeys.shape[1]
    return pl.pallas_call(
        functools.partial(private_kernel, draft=draft, copies=copies, batch=batch),
        grid=(KVH // batch,),
        in_specs=[
            SMEM_SPEC,
            SMEM_SPEC,
            pl.BlockSpec((draft, batch * WIDE), lambda g: (0, g)),
            pl.BlockSpec((draft, batch * HD), lambda g: (0, g)),
            pl.BlockSpec((draft, batch * HD), lambda g: (0, g)),
            pl.BlockSpec((1, slots, batch * HD), lambda g: (0, 0, g)),
            pl.BlockSpec((1, slots, batch * HD), lambda g: (0, 0, g)),
        ],
        out_specs=pl.BlockSpec((batch * copies, draft, MESSAGE), lambda g: (g, 0, 0)),
        out_shape=jax.ShapeDtypeStruct((KVH * copies, draft, MESSAGE), BF16),
        cost_estimate=pl.CostEstimate(
            flops=4 * draft * HEADS * slots * HD,
            transcendentals=draft * HEADS * slots,
            bytes_accessed=4 * slots * KVH * HD,
        ),
        name="private_part",
    )(parents, lengths, queries, dkeys, dvals, pkeys, pvals)


def by_parity(parity, own, twin):
    return (jnp.where(parity == 0, own, twin), jnp.where(parity == 0, twin, own))


def prefix_kernel(
    place_ref, own_ref, twin_ref, k_ref, v_ref, keep_ref, send_ref, own32, twin32, qs, peak, denom, acc
):
    step = pl.program_id(0)
    chips, draft, _ = own_ref.shape
    half = chips * draft
    rows = 2 * half * GROUP
    span = k_ref.shape[1]

    @pl.when(step == 0)
    def _():
        for j in range(chips):
            own32[j * draft : (j + 1) * draft, :] = own_ref[j, :, :WIDE].astype(F32)
            twin32[j * draft : (j + 1) * draft, :] = twin_ref[j, :, :WIDE].astype(F32)
        halves = by_parity(place_ref[1], own32[...], twin32[...])
        for h in range(GROUP):
            for p in range(2):
                at = (2 * h + p) * half
                qs[at : at + half, :] = halves[p][:, h * HD : (h + 1) * HD].astype(BF16)
        head = lax.dot_general(k_ref[0, :HD, :], qs[...], NT, preferred_element_type=F32)
        peak[...] = jnp.max(head, axis=0, keepdims=True) * (SCALE * LOG2E)
        denom[...] = jnp.zeros(denom.shape, F32)
        acc[...] = jnp.zeros(acc.shape, F32)

    scores = lax.dot_general(k_ref[0], qs[...], NT, preferred_element_type=F32)
    weights = jnp.exp2(scores * (SCALE * LOG2E) - peak[...])
    total = denom[...] + jnp.sum(weights.reshape(span // 8, 8, rows), axis=0)
    mixed = acc[...] + lax.dot_general(v_ref[0], weights.astype(BF16), TN, preferred_element_type=F32)
    fits = jnp.max(total) < LIMIT

    @pl.when(fits)
    def _():
        denom[...] = total
        acc[...] = mixed

    @pl.when(jnp.logical_not(fits))
    def _():
        part = 4 * HD

        @pl.loop(0, span // part)
        def _(b):
            block = pl.ds(pl.multiple_of(b * part, part), part)
            scores = lax.dot_general(k_ref[0, block, :], qs[...], NT, preferred_element_type=F32)
            scores = scores * (SCALE * LOG2E)
            old = peak[...]
            new = jnp.maximum(old, jnp.max(scores, axis=0, keepdims=True))
            fade = jnp.exp2(old - new)
            weights = jnp.exp2(scores - new)
            peak[...] = new
            denom[...] = denom[...] * fade + jnp.sum(weights.reshape(part // 8, 8, rows), axis=0)
            acc[...] = acc[...] * fade + lax.dot_general(
                v_ref[0, block, :], weights.astype(BF16), TN, preferred_element_type=F32
            )

    @pl.when(step == pl.num_programs(0) - 1)
    def _():
        total = jnp.sum(denom[...], axis=0, keepdims=True)
        lse = peak[...] * (1.0 / LOG2E) + jnp.log(total)
        mixed = (acc[...] / total).T
        lse = jnp.broadcast_to(lse, (LANES, rows)).T
        lower = place_ref[0] == 0
        split = rows // 2
        keep_ref[:, :HD] = jnp.where(lower, mixed[:split], mixed[split:])
        keep_ref[:, HD:] = jnp.where(lower, lse[:split], lse[split:])
        send_ref[:, :HD] = jnp.where(lower, mixed[split:], mixed[:split])
        send_ref[:, HD:] = jnp.where(lower, lse[split:], lse[:split])


def prefix_part(place, own, twin, keys, values, span):
    chips, draft, _ = own.shape
    half = chips * draft
    rows = 2 * half * GROUP
    shape = jax.ShapeDtypeStruct((rows // 2, HD + LANES), F32)
    whole = pl.BlockSpec(own.shape, lambda i: (0, 0, 0))
    return pl.pallas_call(
        prefix_kernel,
        grid=(keys.shape[1] // span,),
        in_specs=[
            SMEM_SPEC,
            whole,
            whole,
            pl.BlockSpec((1, span, HD), lambda i: (0, i, 0)),
            pl.BlockSpec((1, span, HD), lambda i: (0, i, 0)),
        ],
        out_specs=[pl.BlockSpec((rows // 2, HD + LANES), lambda i: (0, 0))] * 2,
        out_shape=[shape, shape],
        scratch_shapes=[
            pltpu.VMEM((half, WIDE), F32),
            pltpu.VMEM((half, WIDE), F32),
            pltpu.VMEM((rows, HD), BF16),
            pltpu.VMEM((1, rows), F32),
            pltpu.VMEM((8, rows), F32),
            pltpu.VMEM((HD, rows), F32),
        ],
        compiler_params=pltpu.CompilerParams(vmem_limit_bytes=40 << 20),
        cost_estimate=pl.CostEstimate(
            flops=4 * rows * keys.shape[1] * HD,
            transcendentals=rows * keys.shape[1],
            bytes_accessed=4 * keys.shape[1] * HD,
        ),
        name="prefix_part",
    )(place, on_chip(own), on_chip(twin), in_hbm(keys), in_hbm(values))


def join(first, second):
    out_a, lse_a = first[:, :HD], first[:, HD:]
    out_b, lse_b = second[:, :HD], second[:, HD:]
    top = jnp.maximum(lse_a, lse_b)
    scale_a = jnp.exp(lse_a - top)
    scale_b = jnp.exp(lse_b - top)
    both = scale_a + scale_b
    return jnp.concatenate(
        [(scale_a * out_a + scale_b * out_b) / both, top + jnp.log(both)], axis=1
    )


def merge_kernel(
    place_ref, mine_ref, other_ref, own_ref, twin_ref, w_ref, att_ref, wide_ref, own32, twin32, sem
):
    fetch = pltpu.make_async_copy(w_ref.at[:, place_ref[1]], wide_ref, sem)
    fetch.start()
    chips, draft, _ = own_ref.shape
    half = chips * draft
    wide = att_ref.shape[2]
    heads = wide // HD
    first_head = place_ref[2] * heads
    col = pl.multiple_of(first_head * HD, wide)
    for given, held in ((own_ref, own32), (twin_ref, twin32)):
        for j in range(chips):
            part = slice(j * draft, (j + 1) * draft)
            held[part, :wide] = given[j, :, pl.ds(WIDE + col, wide)].astype(F32) + given[
                j, :, pl.ds(2 * WIDE + col, wide)
            ].astype(F32)
            held[part, wide:] = given[j, :, 3 * WIDE :].astype(F32)
    told = by_parity(place_ref[1], own32[...], twin32[...])
    lane = lax.broadcasted_iota(jnp.int32, (half, LANES), 1)
    for h in range(heads):
        at = 3 * (first_head + h)
        mark = (lane >= at) & (lane < at + 3)
        for p in range(2):
            out_p = told[p][:, h * HD : (h + 1) * HD]
            lse_p = jnp.sum(jnp.where(mark, told[p][:, wide:], 0.0), axis=1, keepdims=True)
            part = slice((2 * h + p) * half, (2 * h + p + 1) * half)
            lse_a = mine_ref[part, HD:]
            lse_b = other_ref[part, HD:]
            top = jnp.maximum(jnp.maximum(lse_a, lse_b), lse_p)
            scale_a = jnp.exp(lse_a - top)
            scale_b = jnp.exp(lse_b - top)
            scale_p = jnp.exp(lse_p - top)
            mixed = scale_a * mine_ref[part, :HD] + scale_b * other_ref[part, :HD] + scale_p * out_p
            mixed = (mixed / (scale_a + scale_b + scale_p)).astype(BF16)
            for copy in range(att_ref.shape[0]):
                att_ref[copy, p * half : (p + 1) * half, h * HD : (h + 1) * HD] = mixed
    fetch.wait()


def merge_part(place, mine, other, own, twin, weight):
    chips, draft, _ = own.shape
    half = chips * draft
    _, _, deep, cols = weight.shape
    return pl.pallas_call(
        merge_kernel,
        in_specs=[SMEM_SPEC] + [VMEM_SPEC] * 4 + [pl.BlockSpec(memory_space=pl.ANY)],
        out_specs=[VMEM_SPEC, VMEM_SPEC],
        out_shape=[
            pltpu.VMEM((chips, 2 * half, deep), BF16),
            pltpu.VMEM((chips, deep, cols), BF16),
        ],
        scratch_shapes=[
            pltpu.VMEM((half, deep + LANES), F32),
            pltpu.VMEM((half, deep + LANES), F32),
            pltpu.SemaphoreType.DMA,
        ],
        compiler_params=pltpu.CompilerParams(vmem_limit_bytes=8 << 20),
        cost_estimate=pl.CostEstimate(
            flops=8 * mine.size, transcendentals=mine.size, bytes_accessed=2 * chips * deep * cols
        ),
        name="merge_part",
    )(place, on_chip(mine), on_chip(other), on_chip(own), on_chip(twin), in_hbm(weight))


def matmuls(att_ref, wide_ref):
    return functools.reduce(
        jnp.add,
        [
            jnp.dot(att_ref[i], wide_ref[i], preferred_element_type=F32)
            for i in range(att_ref.shape[0])
        ],
    )


def first_kernel(place_ref, att_ref, wide_ref, w_ref, out_ref, next_ref, sem):
    fetch = pltpu.make_async_copy(w_ref.at[:, 1 - place_ref[1]], next_ref, sem)
    fetch.start()
    out_ref[...] = matmuls(att_ref, wide_ref)
    fetch.wait()


def second_kernel(part_ref, att_ref, wide_ref, out_ref):
    total = part_ref[...] + matmuls(att_ref, wide_ref)
    owners, draft, _ = out_ref.shape
    for s in range(owners):
        at = ((s % 2) * (owners // 2) + s // 2) * draft
        out_ref[s] = total[at : at + draft].astype(BF16)


def project_own(place, att, wide, weight):
    chips, rows, deep = att.shape
    cols = weight.shape[3]
    return pl.pallas_call(
        first_kernel,
        in_specs=[SMEM_SPEC, VMEM_SPEC, VMEM_SPEC, pl.BlockSpec(memory_space=pl.ANY)],
        out_specs=[VMEM_SPEC, VMEM_SPEC],
        out_shape=[pltpu.VMEM((rows, cols), F32), pltpu.VMEM((chips, deep, cols), BF16)],
        scratch_shapes=[pltpu.SemaphoreType.DMA],
        compiler_params=pltpu.CompilerParams(vmem_limit_bytes=8 << 20),
        cost_estimate=pl.CostEstimate(
            flops=2 * rows * deep * chips * cols,
            transcendentals=0,
            bytes_accessed=2 * deep * chips * cols,
        ),
        name="project_own",
    )(place, on_chip(att), on_chip(wide), in_hbm(weight))


def project_twin(part, att, wide, owners):
    chips, rows, deep = att.shape
    cols = wide.shape[2]
    return pl.pallas_call(
        second_kernel,
        in_specs=[VMEM_SPEC, VMEM_SPEC, VMEM_SPEC],
        out_specs=VMEM_SPEC,
        out_shape=pltpu.VMEM((owners, rows // owners, cols), BF16),
        compiler_params=pltpu.CompilerParams(vmem_limit_bytes=8 << 20),
        cost_estimate=pl.CostEstimate(
            flops=2 * rows * deep * chips * cols, transcendentals=0, bytes_accessed=0
        ),
        name="project_twin",
    )(on_chip(part), on_chip(att), on_chip(wide))


def shards(
    queries,
    draft_keys,
    draft_values,
    parents,
    private_keys,
    private_values,
    priv_lengths,
    prefix_keys,
    prefix_values,
    out_weight,
):
    own_rows = queries.shape[0]
    seq = lax.axis_size("seq")
    chips = seq // 2
    blocks = seq // KVH
    device = lax.axis_index("seq")
    rank = device % blocks
    top_bit = blocks.bit_length() - 2
    place = jnp.stack([(rank >> top_bit) & 1, device % 2, rank]).astype(jnp.int32)
    members = [list(range(c, seq, 2)) for c in range(2)]

    def from_partner(array, bit):
        return lax.ppermute(array, "seq", [(i, i ^ 1 << bit) for i in range(seq)])

    def among_members(array):
        return lax.all_to_all(
            array, "seq", split_axis=0, concat_axis=0, axis_index_groups=members, tiled=True
        )

    message = private_part(
        parents,
        priv_lengths,
        queries,
        draft_keys,
        draft_values,
        in_hbm(private_keys),
        in_hbm(private_values),
        blocks // 2,
        KVH // 2,
    )
    own = among_members(message)
    twin = from_partner(own, 0)

    span = min(4096, prefix_keys.shape[1])
    mine, gone = prefix_part(place, own, twin, prefix_keys, prefix_values, span)
    other = from_partner(gone, top_bit)
    for level in range(top_bit - 1, -1, -1):
        held = join(mine, other)
        half = held.shape[0] // 2
        at = (rank >> level) & 1
        mine = lax.dynamic_slice_in_dim(held, at * half, half, 0)
        other = from_partner(lax.dynamic_slice_in_dim(held, (1 - at) * half, half, 0), level)

    weight = out_weight.reshape(chips, 2, -1, out_weight.shape[1])
    copies, wide = merge_part(place, mine, other, own, twin, weight)
    same = among_members(copies)
    twin = from_partner(same, 0)
    part, wide = project_own(place, same, wide, weight)
    pieces = project_twin(part, twin, wide, seq)
    done = lax.all_to_all(pieces, "seq", split_axis=0, concat_axis=0, tiled=True)
    return done.transpose(1, 0, 2).reshape(own_rows, -1).astype(F32)


def solution(mesh):
    in_specs = (
        P(("groups", "seq"), None),
        P(("groups", "seq"), None),
        P(("groups", "seq"), None),
        P(("groups", "seq")),
        P(("groups", "seq"), None, None),
        P(("groups", "seq"), None, None),
        P(("groups", "seq")),
        P(("groups", "seq"), None, None),
        P(("groups", "seq"), None, None),
        P(None, "seq"),
    )
    out_specs = P(("groups", "seq"), None)

    return jax.shard_map(shards, mesh=mesh, in_specs=in_specs, out_specs=out_specs, check_vma=False)
```

```python
import functools

import jax
import jax.numpy as jnp
from jax import lax
from jax.experimental import pallas as pl
from jax.experimental.pallas import tpu as pltpu
from jax.sharding import PartitionSpec as P


HEADS = 64
KVH = 8
HD = 128
GROUP = HEADS // KVH
SCALE = HD ** (-0.5)
LOG2E = 1.4426950408889634
LANES = 128
NEG = -1e30
LIMIT = 2.0**100
WIDE = GROUP * HD
MESSAGE = 3 * WIDE + LANES
NT = (((1,), (1,)), ((), ()))
TN = (((0,), (0,)), ((), ()))
F32 = jnp.float32
BF16 = jnp.bfloat16


def in_hbm(array):
    return pltpu.with_memory_space_constraint(array, pltpu.HBM)


def on_chip(array):
    return pltpu.with_memory_space_constraint(array, pltpu.VMEM)


VMEM_SPEC = pl.BlockSpec(memory_space=pltpu.VMEM)
SMEM_SPEC = pl.BlockSpec(memory_space=pltpu.SMEM)


def private_kernel(
    par_ref, len_ref, q_ref, dk_ref, dv_ref, k_ref, v_ref, out_ref, *, draft, copies, batch
):
    rows = GROUP * draft
    slots = k_ref.shape[1]
    seen = []
    for i in range(draft):
        bits = jnp.int32(1 << i)
        for j in range(i):
            bits = bits | jnp.where(par_ref[i] == j, seen[j], 0)
        seen.append(bits)
    row = lax.broadcasted_iota(jnp.int32, (rows, LANES), 0) % draft
    lane = lax.broadcasted_iota(jnp.int32, (rows, LANES), 1)
    mask = jnp.zeros((rows, LANES), jnp.int32)
    for i in range(draft):
        mask = jnp.where(row == i, seen[i], mask)
    shown = (lane < draft) & ((lax.shift_right_logical(mask, jnp.minimum(lane, 31)) & 1) == 1)
    live = lax.broadcasted_iota(jnp.int32, (rows, slots), 1) < len_ref[0]
    fill = jnp.zeros((LANES - draft, HD), F32)
    stat_lane = lax.broadcasted_iota(jnp.int32, (draft, LANES), 1)
    groups = range(batch)
    queries = []
    for g in groups:
        q = q_ref[:, g * WIDE : (g + 1) * WIDE]
        for copy in range(copies):
            out_ref[g * copies + copy, :, :WIDE] = q
        q32 = q.astype(F32)
        queries.append(
            jnp.concatenate([q32[:, h * HD : (h + 1) * HD] for h in range(GROUP)], axis=0).astype(BF16)
        )
    cols = [slice(g * HD, (g + 1) * HD) for g in groups]
    scores = [
        lax.dot_general(queries[g], k_ref[0, :, cols[g]], NT, preferred_element_type=F32) for g in groups
    ]
    trees = []
    for g in groups:
        dkey = jnp.concatenate([dk_ref[:, cols[g]].astype(F32), fill], axis=0).astype(BF16)
        trees.append(lax.dot_general(queries[g], dkey, NT, preferred_element_type=F32))
    for g in groups:
        score = jnp.where(live, scores[g] * SCALE, NEG)
        tree = jnp.where(shown, trees[g] * SCALE, NEG)
        tiles = [score[:, j : j + LANES] for j in range(0, slots, LANES)] + [tree]
        peak = jnp.max(functools.reduce(jnp.maximum, tiles), axis=1, keepdims=True)
        tiles = [jnp.exp(tile - peak) for tile in tiles]
        denom = jnp.sum(functools.reduce(jnp.add, tiles), axis=1, keepdims=True)
        weights = jnp.concatenate([tile.astype(BF16) for tile in tiles[:-1]], axis=1)
        dval = jnp.concatenate([dv_ref[:, cols[g]].astype(F32), fill], axis=0).astype(BF16)
        mixture = jnp.dot(weights, v_ref[0, :, cols[g]], preferred_element_type=F32)
        mixture = mixture + jnp.dot(tiles[-1].astype(BF16), dval, preferred_element_type=F32)
        mixture = mixture / denom
        coarse = mixture.astype(BF16).astype(F32)
        fine = mixture - coarse
        lse = peak + jnp.log(denom)
        first = lse.astype(BF16).astype(F32)
        second = (lse - first).astype(BF16).astype(F32)
        third = lse - first - second
        stats = jnp.zeros((draft, LANES), F32)
        for copy in range(copies):
            at = g * copies + copy
            for h in range(GROUP):
                part = slice(h * draft, (h + 1) * draft)
                out_ref[at, :, WIDE + h * HD : WIDE + (h + 1) * HD] = coarse[part].astype(BF16)
                out_ref[at, :, 2 * WIDE + h * HD : 2 * WIDE + (h + 1) * HD] = fine[part].astype(BF16)
                if copy == 0:
                    for t, term in enumerate((first, second, third)):
                        stats = jnp.where(stat_lane == 3 * h + t, term[part], stats)
            out_ref[at, :, 3 * WIDE :] = stats.astype(BF16)


def private_part(parents, lengths, queries, dkeys, dvals, pkeys, pvals, copies, batch):
    draft = queries.shape[0]
    slots = pkeys.shape[1]
    return pl.pallas_call(
        functools.partial(private_kernel, draft=draft, copies=copies, batch=batch),
        grid=(KVH // batch,),
        in_specs=[
            SMEM_SPEC,
            SMEM_SPEC,
            pl.BlockSpec((draft, batch * WIDE), lambda g: (0, g)),
            pl.BlockSpec((draft, batch * HD), lambda g: (0, g)),
            pl.BlockSpec((draft, batch * HD), lambda g: (0, g)),
            pl.BlockSpec((1, slots, batch * HD), lambda g: (0, 0, g)),
            pl.BlockSpec((1, slots, batch * HD), lambda g: (0, 0, g)),
        ],
        out_specs=pl.BlockSpec((batch * copies, draft, MESSAGE), lambda g: (g, 0, 0)),
        out_shape=jax.ShapeDtypeStruct((KVH * copies, draft, MESSAGE), BF16),
        cost_estimate=pl.CostEstimate(
            flops=4 * draft * HEADS * slots * HD,
            transcendentals=draft * HEADS * slots,
            bytes_accessed=4 * slots * KVH * HD,
        ),
        name="private_part",
    )(parents, lengths, queries, dkeys, dvals, pkeys, pvals)


def by_parity(parity, own, twin):
    return (jnp.where(parity == 0, own, twin), jnp.where(parity == 0, twin, own))


def prefix_kernel(
    place_ref,
    own_ref,
    twin_ref,
    k_ref,
    v_ref,
    w_ref,
    keep_ref,
    send_ref,
    wide_ref,
    own32,
    twin32,
    qs,
    peak,
    denom,
    acc,
    sem,
):
    step = pl.program_id(0)
    chips, draft, _ = own_ref.shape
    half = chips * draft
    rows = 2 * half * GROUP
    span = k_ref.shape[1]
    fetch = pltpu.make_async_copy(w_ref, wide_ref, sem)

    @pl.when(step == 0)
    def _():
        fetch.start()
        for j in range(chips):
            own32[j * draft : (j + 1) * draft, :] = own_ref[j, :, :WIDE].astype(F32)
            twin32[j * draft : (j + 1) * draft, :] = twin_ref[j, :, :WIDE].astype(F32)
        halves = by_parity(place_ref[1], own32[...], twin32[...])
        for h in range(GROUP):
            for p in range(2):
                at = (2 * h + p) * half
                qs[at : at + half, :] = halves[p][:, h * HD : (h + 1) * HD].astype(BF16)
        head = lax.dot_general(k_ref[0, :HD, :], qs[...], NT, preferred_element_type=F32)
        peak[...] = jnp.max(head, axis=0, keepdims=True) * (SCALE * LOG2E)
        denom[...] = jnp.zeros(denom.shape, F32)
        acc[...] = jnp.zeros(acc.shape, F32)

    scores = lax.dot_general(k_ref[0], qs[...], NT, preferred_element_type=F32)
    weights = jnp.exp2(scores * (SCALE * LOG2E) - peak[...])
    total = denom[...] + jnp.sum(weights.reshape(span // 8, 8, rows), axis=0)
    mixed = acc[...] + lax.dot_general(v_ref[0], weights.astype(BF16), TN, preferred_element_type=F32)
    fits = jnp.max(total) < LIMIT

    @pl.when(fits)
    def _():
        denom[...] = total
        acc[...] = mixed

    @pl.when(jnp.logical_not(fits))
    def _():
        part = 4 * HD

        @pl.loop(0, span // part)
        def _(b):
            block = pl.ds(pl.multiple_of(b * part, part), part)
            scores = lax.dot_general(k_ref[0, block, :], qs[...], NT, preferred_element_type=F32)
            scores = scores * (SCALE * LOG2E)
            old = peak[...]
            new = jnp.maximum(old, jnp.max(scores, axis=0, keepdims=True))
            fade = jnp.exp2(old - new)
            weights = jnp.exp2(scores - new)
            peak[...] = new
            denom[...] = denom[...] * fade + jnp.sum(weights.reshape(part // 8, 8, rows), axis=0)
            acc[...] = acc[...] * fade + lax.dot_general(
                v_ref[0, block, :], weights.astype(BF16), TN, preferred_element_type=F32
            )

    @pl.when(step == pl.num_programs(0) - 1)
    def _():
        total = jnp.sum(denom[...], axis=0, keepdims=True)
        lse = peak[...] * (1.0 / LOG2E) + jnp.log(total)
        mixed = (acc[...] / total).T
        lse = jnp.broadcast_to(lse, (LANES, rows)).T
        lower = place_ref[0] == 0
        split = rows // 2
        keep_ref[:, :HD] = jnp.where(lower, mixed[:split], mixed[split:])
        keep_ref[:, HD:] = jnp.where(lower, lse[:split], lse[split:])
        send_ref[:, :HD] = jnp.where(lower, mixed[split:], mixed[:split])
        send_ref[:, HD:] = jnp.where(lower, lse[split:], lse[:split])
        fetch.wait()


def prefix_part(place, own, twin, keys, values, weight, span):
    chips, draft, _ = own.shape
    half = chips * draft
    rows = 2 * half * GROUP
    shape = jax.ShapeDtypeStruct((rows // 2, HD + LANES), F32)
    whole = pl.BlockSpec(own.shape, lambda i: (0, 0, 0))
    return pl.pallas_call(
        prefix_kernel,
        grid=(keys.shape[1] // span,),
        in_specs=[
            SMEM_SPEC,
            whole,
            whole,
            pl.BlockSpec((1, span, HD), lambda i: (0, i, 0)),
            pl.BlockSpec((1, span, HD), lambda i: (0, i, 0)),
            pl.BlockSpec(memory_space=pl.ANY),
        ],
        out_specs=[pl.BlockSpec((rows // 2, HD + LANES), lambda i: (0, 0))] * 2 + [VMEM_SPEC],
        out_shape=[shape, shape, pltpu.VMEM(weight.shape, BF16)],
        scratch_shapes=[
            pltpu.VMEM((half, WIDE), F32),
            pltpu.VMEM((half, WIDE), F32),
            pltpu.VMEM((rows, HD), BF16),
            pltpu.VMEM((1, rows), F32),
            pltpu.VMEM((8, rows), F32),
            pltpu.VMEM((HD, rows), F32),
            pltpu.SemaphoreType.DMA,
        ],
        compiler_params=pltpu.CompilerParams(vmem_limit_bytes=40 << 20),
        cost_estimate=pl.CostEstimate(
            flops=4 * rows * keys.shape[1] * HD,
            transcendentals=rows * keys.shape[1],
            bytes_accessed=4 * keys.shape[1] * HD,
        ),
        name="prefix_part",
    )(place, on_chip(own), on_chip(twin), in_hbm(keys), in_hbm(values), in_hbm(weight))


def join(first, second):
    out_a, lse_a = first[:, :HD], first[:, HD:]
    out_b, lse_b = second[:, :HD], second[:, HD:]
    top = jnp.maximum(lse_a, lse_b)
    scale_a = jnp.exp(lse_a - top)
    scale_b = jnp.exp(lse_b - top)
    both = scale_a + scale_b
    return jnp.concatenate(
        [(scale_a * out_a + scale_b * out_b) / both, top + jnp.log(both)], axis=1
    )


def merge_kernel(
    place_ref, mine_ref, other_ref, own_ref, twin_ref, att_ref, own32, twin32
):
    chips, draft, _ = own_ref.shape
    half = chips * draft
    wide = att_ref.shape[2]
    heads = wide // HD
    first_head = place_ref[2] * heads
    col = pl.multiple_of(first_head * HD, wide)
    for given, held in ((own_ref, own32), (twin_ref, twin32)):
        for j in range(chips):
            part = slice(j * draft, (j + 1) * draft)
            held[part, :wide] = given[j, :, pl.ds(WIDE + col, wide)].astype(F32) + given[
                j, :, pl.ds(2 * WIDE + col, wide)
            ].astype(F32)
            held[part, wide:] = given[j, :, 3 * WIDE :].astype(F32)
    told = by_parity(place_ref[1], own32[...], twin32[...])
    lane = lax.broadcasted_iota(jnp.int32, (half, LANES), 1)
    for h in range(heads):
        at = 3 * (first_head + h)
        mark = (lane >= at) & (lane < at + 3)
        for p in range(2):
            out_p = told[p][:, h * HD : (h + 1) * HD]
            lse_p = jnp.sum(jnp.where(mark, told[p][:, wide:], 0.0), axis=1, keepdims=True)
            part = slice((2 * h + p) * half, (2 * h + p + 1) * half)
            lse_a = mine_ref[part, HD:]
            lse_b = other_ref[part, HD:]
            top = jnp.maximum(jnp.maximum(lse_a, lse_b), lse_p)
            scale_a = jnp.exp(lse_a - top)
            scale_b = jnp.exp(lse_b - top)
            scale_p = jnp.exp(lse_p - top)
            mixed = scale_a * mine_ref[part, :HD] + scale_b * other_ref[part, :HD] + scale_p * out_p
            mixed = (mixed / (scale_a + scale_b + scale_p)).astype(BF16)
            for copy in range(att_ref.shape[0]):
                att_ref[copy, p * half : (p + 1) * half, h * HD : (h + 1) * HD] = mixed


def merge_part(place, mine, other, own, twin, deep):
    chips, draft, _ = own.shape
    half = chips * draft
    return pl.pallas_call(
        merge_kernel,
        in_specs=[SMEM_SPEC] + [VMEM_SPEC] * 4,
        out_specs=VMEM_SPEC,
        out_shape=pltpu.VMEM((chips, 2 * half, deep), BF16),
        scratch_shapes=[
            pltpu.VMEM((half, deep + LANES), F32),
            pltpu.VMEM((half, deep + LANES), F32),
        ],
        compiler_params=pltpu.CompilerParams(vmem_limit_bytes=8 << 20),
        cost_estimate=pl.CostEstimate(
            flops=8 * mine.size, transcendentals=mine.size, bytes_accessed=0
        ),
        name="merge_part",
    )(place, on_chip(mine), on_chip(other), on_chip(own), on_chip(twin))


def matmuls(att_ref, wide_ref, parity):
    return functools.reduce(
        jnp.add,
        [
            jnp.dot(att_ref[i], wide_ref[i, parity], preferred_element_type=F32)
            for i in range(att_ref.shape[0])
        ],
    )


def first_kernel(place_ref, att_ref, wide_ref, out_ref):
    out_ref[...] = matmuls(att_ref, wide_ref, place_ref[1])


def second_kernel(place_ref, part_ref, att_ref, wide_ref, out_ref):
    total = part_ref[...] + matmuls(att_ref, wide_ref, 1 - place_ref[1])
    owners, draft, _ = out_ref.shape
    for s in range(owners):
        at = ((s % 2) * (owners // 2) + s // 2) * draft
        out_ref[s] = total[at : at + draft].astype(BF16)


def project_own(place, att, wide):
    chips, rows, deep = att.shape
    cols = wide.shape[3]
    return pl.pallas_call(
        first_kernel,
        in_specs=[SMEM_SPEC, VMEM_SPEC, VMEM_SPEC],
        out_specs=VMEM_SPEC,
        out_shape=pltpu.VMEM((rows, cols), F32),
        compiler_params=pltpu.CompilerParams(vmem_limit_bytes=8 << 20),
        cost_estimate=pl.CostEstimate(
            flops=2 * rows * deep * chips * cols, transcendentals=0, bytes_accessed=0
        ),
        name="project_own",
    )(place, on_chip(att), on_chip(wide))


def project_twin(place, part, att, wide, owners):
    chips, rows, deep = att.shape
    cols = wide.shape[3]
    return pl.pallas_call(
        second_kernel,
        in_specs=[SMEM_SPEC, VMEM_SPEC, VMEM_SPEC, VMEM_SPEC],
        out_specs=VMEM_SPEC,
        out_shape=pltpu.VMEM((owners, rows // owners, cols), BF16),
        compiler_params=pltpu.CompilerParams(vmem_limit_bytes=8 << 20),
        cost_estimate=pl.CostEstimate(
            flops=2 * rows * deep * chips * cols, transcendentals=0, bytes_accessed=0
        ),
        name="project_twin",
    )(place, on_chip(part), on_chip(att), on_chip(wide))


def shards(
    queries,
    draft_keys,
    draft_values,
    parents,
    private_keys,
    private_values,
    priv_lengths,
    prefix_keys,
    prefix_values,
    out_weight,
):
    own_rows = queries.shape[0]
    seq = lax.axis_size("seq")
    chips = seq // 2
    blocks = seq // KVH
    device = lax.axis_index("seq")
    rank = device % blocks
    top_bit = blocks.bit_length() - 2
    place = jnp.stack([(rank >> top_bit) & 1, device % 2, rank]).astype(jnp.int32)
    members = [list(range(c, seq, 2)) for c in range(2)]

    def from_partner(array, bit):
        return lax.ppermute(array, "seq", [(i, i ^ 1 << bit) for i in range(seq)])

    def among_members(array):
        return lax.all_to_all(
            array, "seq", split_axis=0, concat_axis=0, axis_index_groups=members, tiled=True
        )

    message = private_part(
        parents,
        priv_lengths,
        queries,
        draft_keys,
        draft_values,
        in_hbm(private_keys),
        in_hbm(private_values),
        blocks // 2,
        KVH // 2,
    )
    own = among_members(message)
    twin = from_partner(own, 0)

    span = min(4096, prefix_keys.shape[1])
    weight = out_weight.reshape(chips, 2, -1, out_weight.shape[1])
    mine, gone, wide = prefix_part(place, own, twin, prefix_keys, prefix_values, weight, span)
    other = from_partner(gone, top_bit)
    for level in range(top_bit - 1, -1, -1):
        held = join(mine, other)
        half = held.shape[0] // 2
        at = (rank >> level) & 1
        mine = lax.dynamic_slice_in_dim(held, at * half, half, 0)
        other = from_partner(lax.dynamic_slice_in_dim(held, (1 - at) * half, half, 0), level)

    copies = merge_part(place, mine, other, own, twin, weight.shape[2])
    same = among_members(copies)
    twin = from_partner(same, 0)
    part = project_own(place, same, wide)
    pieces = project_twin(place, part, twin, wide, seq)
    done = lax.all_to_all(pieces, "seq", split_axis=0, concat_axis=0, tiled=True)
    return done.transpose(1, 0, 2).reshape(own_rows, -1).astype(F32)


def solution(mesh):
    in_specs = (
        P(("groups", "seq"), None),
        P(("groups", "seq"), None),
        P(("groups", "seq"), None),
        P(("groups", "seq")),
        P(("groups", "seq"), None, None),
        P(("groups", "seq"), None, None),
        P(("groups", "seq")),
        P(("groups", "seq"), None, None),
        P(("groups", "seq"), None, None),
        P(None, "seq"),
    )
    out_specs = P(("groups", "seq"), None)

    return jax.shard_map(shards, mesh=mesh, in_specs=in_specs, out_specs=out_specs, check_vma=False)
```

```python
import functools

import jax
import jax.numpy as jnp
from jax import lax
from jax.experimental import pallas as pl
from jax.experimental.pallas import tpu as pltpu
from jax.sharding import PartitionSpec as P

HEADS = 64
KVH = 8
HD = 128
GROUP = HEADS // KVH
SCALE = HD ** (-0.5)
LOG2E = 1.4426950408889634
LANES = 128
NEG = -1e30
LIMIT = 2.0**100
WIDE = GROUP * HD
MESSAGE = 3 * WIDE + LANES
NT = (((1,), (1,)), ((), ()))
TN = (((0,), (0,)), ((), ()))
F32 = jnp.float32
BF16 = jnp.bfloat16


def in_hbm(array):
    return pltpu.with_memory_space_constraint(array, pltpu.HBM)


def on_chip(array):
    return pltpu.with_memory_space_constraint(array, pltpu.VMEM)


VMEM_SPEC = pl.BlockSpec(memory_space=pltpu.VMEM)
SMEM_SPEC = pl.BlockSpec(memory_space=pltpu.SMEM)


def private_kernel(
    par_ref, len_ref, q_ref, dk_ref, dv_ref, k_ref, v_ref, out_ref, *, draft, copies, batch
):
    rows = GROUP * draft
    slots = k_ref.shape[1]
    seen = []
    for i in range(draft):
        bits = jnp.int32(1 << i)
        for j in range(i):
            bits = bits | jnp.where(par_ref[i] == j, seen[j], 0)
        seen.append(bits)
    row = lax.broadcasted_iota(jnp.int32, (rows, LANES), 0) % draft
    lane = lax.broadcasted_iota(jnp.int32, (rows, LANES), 1)
    mask = jnp.zeros((rows, LANES), jnp.int32)
    for i in range(draft):
        mask = jnp.where(row == i, seen[i], mask)
    shown = (lane < draft) & ((lax.shift_right_logical(mask, jnp.minimum(lane, 31)) & 1) == 1)
    live = lax.broadcasted_iota(jnp.int32, (rows, slots), 1) < len_ref[0]
    fill = jnp.zeros((LANES - draft, HD), F32)
    stat_lane = lax.broadcasted_iota(jnp.int32, (draft, LANES), 1)
    groups = range(batch)
    queries = []
    for g in groups:
        q = q_ref[:, g * WIDE : (g + 1) * WIDE]
        for copy in range(copies):
            out_ref[g * copies + copy, :, :WIDE] = q
        q32 = q.astype(F32)
        queries.append(
            jnp.concatenate([q32[:, h * HD : (h + 1) * HD] for h in range(GROUP)], axis=0).astype(BF16)
        )
    cols = [slice(g * HD, (g + 1) * HD) for g in groups]
    scores = [
        lax.dot_general(queries[g], k_ref[0, :, cols[g]], NT, preferred_element_type=F32) for g in groups
    ]
    trees = []
    for g in groups:
        dkey = jnp.concatenate([dk_ref[:, cols[g]].astype(F32), fill], axis=0).astype(BF16)
        trees.append(lax.dot_general(queries[g], dkey, NT, preferred_element_type=F32))
    for g in groups:
        score = jnp.where(live, scores[g] * SCALE, NEG)
        tree = jnp.where(shown, trees[g] * SCALE, NEG)
        tiles = [score[:, j : j + LANES] for j in range(0, slots, LANES)] + [tree]
        peak = jnp.max(functools.reduce(jnp.maximum, tiles), axis=1, keepdims=True)
        tiles = [jnp.exp(tile - peak) for tile in tiles]
        denom = jnp.sum(functools.reduce(jnp.add, tiles), axis=1, keepdims=True)
        weights = jnp.concatenate([tile.astype(BF16) for tile in tiles[:-1]], axis=1)
        dval = jnp.concatenate([dv_ref[:, cols[g]].astype(F32), fill], axis=0).astype(BF16)
        mixture = jnp.dot(weights, v_ref[0, :, cols[g]], preferred_element_type=F32)
        mixture = mixture + jnp.dot(tiles[-1].astype(BF16), dval, preferred_element_type=F32)
        mixture = mixture / denom
        coarse = mixture.astype(BF16).astype(F32)
        fine = mixture - coarse
        lse = peak + jnp.log(denom)
        first = lse.astype(BF16).astype(F32)
        second = (lse - first).astype(BF16).astype(F32)
        third = lse - first - second
        stats = jnp.zeros((draft, LANES), F32)
        for copy in range(copies):
            at = g * copies + copy
            for h in range(GROUP):
                part = slice(h * draft, (h + 1) * draft)
                out_ref[at, :, WIDE + h * HD : WIDE + (h + 1) * HD] = coarse[part].astype(BF16)
                out_ref[at, :, 2 * WIDE + h * HD : 2 * WIDE + (h + 1) * HD] = fine[part].astype(BF16)
                if copy == 0:
                    for t, term in enumerate((first, second, third)):
                        stats = jnp.where(stat_lane == 3 * h + t, term[part], stats)
            out_ref[at, :, 3 * WIDE :] = stats.astype(BF16)


def private_part(parents, lengths, queries, dkeys, dvals, pkeys, pvals, copies, batch):
    draft = queries.shape[0]
    slots = pkeys.shape[1]
    return pl.pallas_call(
        functools.partial(private_kernel, draft=draft, copies=copies, batch=batch),
        grid=(KVH // batch,),
        in_specs=[
            SMEM_SPEC,
            SMEM_SPEC,
            pl.BlockSpec((draft, batch * WIDE), lambda g: (0, g)),
            pl.BlockSpec((draft, batch * HD), lambda g: (0, g)),
            pl.BlockSpec((draft, batch * HD), lambda g: (0, g)),
            pl.BlockSpec((1, slots, batch * HD), lambda g: (0, 0, g)),
            pl.BlockSpec((1, slots, batch * HD), lambda g: (0, 0, g)),
        ],
        out_specs=pl.BlockSpec((batch * copies, draft, MESSAGE), lambda g: (g, 0, 0)),
        out_shape=jax.ShapeDtypeStruct((KVH * copies, draft, MESSAGE), BF16),
        cost_estimate=pl.CostEstimate(
            flops=4 * draft * HEADS * slots * HD,
            transcendentals=draft * HEADS * slots,
            bytes_accessed=4 * slots * KVH * HD,
        ),
        name="private_part",
    )(parents, lengths, queries, dkeys, dvals, pkeys, pvals)


def by_parity(parity, own, twin):
    return (jnp.where(parity == 0, own, twin), jnp.where(parity == 0, twin, own))


def prefix_kernel(
    place_ref,
    own_ref,
    twin_ref,
    k_ref,
    v_ref,
    w_ref,
    keep_ref,
    send_ref,
    wide_ref,
    own32,
    twin32,
    qs,
    peak,
    denom,
    acc,
    sem,
):
    step = pl.program_id(0)
    chips, draft, _ = own_ref.shape
    half = chips * draft
    rows = 2 * half * GROUP
    span = k_ref.shape[1]
    fetch = pltpu.make_async_copy(w_ref, wide_ref, sem)

    @pl.when(step == 0)
    def _():
        fetch.start()
        for j in range(chips):
            own32[j * draft : (j + 1) * draft, :] = own_ref[j, :, :WIDE].astype(F32)
            twin32[j * draft : (j + 1) * draft, :] = twin_ref[j, :, :WIDE].astype(F32)
        halves = by_parity(place_ref[1], own32[...], twin32[...])
        for h in range(GROUP):
            for p in range(2):
                at = (2 * h + p) * half
                qs[at : at + half, :] = halves[p][:, h * HD : (h + 1) * HD].astype(BF16)
        head = lax.dot_general(k_ref[0, :HD, :], qs[...], NT, preferred_element_type=F32)
        peak[...] = jnp.max(head, axis=0, keepdims=True) * (SCALE * LOG2E)
        denom[...] = jnp.zeros(denom.shape, F32)
        acc[...] = jnp.zeros(acc.shape, F32)

    scores = lax.dot_general(k_ref[0], qs[...], NT, preferred_element_type=F32)
    weights = jnp.exp2(scores * (SCALE * LOG2E) - peak[...])
    total = denom[...] + jnp.sum(weights.reshape(span // 8, 8, rows), axis=0)
    mixed = acc[...] + lax.dot_general(v_ref[0], weights.astype(BF16), TN, preferred_element_type=F32)
    fits = jnp.max(total) < LIMIT

    @pl.when(fits)
    def _():
        denom[...] = total
        acc[...] = mixed

    @pl.when(jnp.logical_not(fits))
    def _():
        part = 4 * HD

        @pl.loop(0, span // part)
        def _(b):
            block = pl.ds(pl.multiple_of(b * part, part), part)
            scores = lax.dot_general(k_ref[0, block, :], qs[...], NT, preferred_element_type=F32)
            scores = scores * (SCALE * LOG2E)
            old = peak[...]
            new = jnp.maximum(old, jnp.max(scores, axis=0, keepdims=True))
            fade = jnp.exp2(old - new)
            weights = jnp.exp2(scores - new)
            peak[...] = new
            denom[...] = denom[...] * fade + jnp.sum(weights.reshape(part // 8, 8, rows), axis=0)
            acc[...] = acc[...] * fade + lax.dot_general(
                v_ref[0, block, :], weights.astype(BF16), TN, preferred_element_type=F32
            )

    @pl.when(step == pl.num_programs(0) - 1)
    def _():
        total = jnp.sum(denom[...], axis=0, keepdims=True)
        lse = peak[...] * (1.0 / LOG2E) + jnp.log(total)
        mixed = (acc[...] / total).T
        lse = jnp.broadcast_to(lse, (LANES, rows)).T
        lower = place_ref[0] == 0
        split = rows // 2
        keep_ref[:, :HD] = jnp.where(lower, mixed[:split], mixed[split:])
        keep_ref[:, HD:] = jnp.where(lower, lse[:split], lse[split:])
        send_ref[:, :HD] = jnp.where(lower, mixed[split:], mixed[:split])
        send_ref[:, HD:] = jnp.where(lower, lse[split:], lse[:split])
        fetch.wait()


def prefix_part(place, own, twin, keys, values, weight, span):
    chips, draft, _ = own.shape
    half = chips * draft
    rows = 2 * half * GROUP
    shape = jax.ShapeDtypeStruct((rows // 2, HD + LANES), F32)
    whole = pl.BlockSpec(own.shape, lambda i: (0, 0, 0))
    return pl.pallas_call(
        prefix_kernel,
        grid=(keys.shape[1] // span,),
        in_specs=[
            SMEM_SPEC,
            whole,
            whole,
            pl.BlockSpec((1, span, HD), lambda i: (0, i, 0)),
            pl.BlockSpec((1, span, HD), lambda i: (0, i, 0)),
            pl.BlockSpec(memory_space=pl.ANY),
        ],
        out_specs=[pl.BlockSpec((rows // 2, HD + LANES), lambda i: (0, 0))] * 2 + [VMEM_SPEC],
        out_shape=[shape, shape, pltpu.VMEM(weight.shape, BF16)],
        scratch_shapes=[
            pltpu.VMEM((half, WIDE), F32),
            pltpu.VMEM((half, WIDE), F32),
            pltpu.VMEM((rows, HD), BF16),
            pltpu.VMEM((1, rows), F32),
            pltpu.VMEM((8, rows), F32),
            pltpu.VMEM((HD, rows), F32),
            pltpu.SemaphoreType.DMA,
        ],
        compiler_params=pltpu.CompilerParams(vmem_limit_bytes=40 << 20),
        cost_estimate=pl.CostEstimate(
            flops=4 * rows * keys.shape[1] * HD,
            transcendentals=rows * keys.shape[1],
            bytes_accessed=4 * keys.shape[1] * HD,
        ),
        name="prefix_part",
    )(place, on_chip(own), on_chip(twin), in_hbm(keys), in_hbm(values), in_hbm(weight))


def join(first, second):
    out_a, lse_a = first[:, :HD], first[:, HD:]
    out_b, lse_b = second[:, :HD], second[:, HD:]
    top = jnp.maximum(lse_a, lse_b)
    scale_a = jnp.exp(lse_a - top)
    scale_b = jnp.exp(lse_b - top)
    both = scale_a + scale_b
    return jnp.concatenate(
        [(scale_a * out_a + scale_b * out_b) / both, top + jnp.log(both)], axis=1
    )


def merge_kernel(
    place_ref, mine_ref, other_ref, own_ref, twin_ref, att_ref, own32, twin32
):
    chips, draft, _ = own_ref.shape
    half = chips * draft
    wide = att_ref.shape[1]
    heads = wide // HD
    first_head = place_ref[2] * heads
    col = pl.multiple_of(first_head * HD, wide)
    for given, held in ((own_ref, own32), (twin_ref, twin32)):
        for j in range(chips):
            part = slice(j * draft, (j + 1) * draft)
            held[part, :wide] = given[j, :, pl.ds(WIDE + col, wide)].astype(F32) + given[
                j, :, pl.ds(2 * WIDE + col, wide)
            ].astype(F32)
            held[part, wide:] = given[j, :, 3 * WIDE :].astype(F32)
    told = by_parity(place_ref[1], own32[...], twin32[...])
    lane = lax.broadcasted_iota(jnp.int32, (half, LANES), 1)
    for h in range(heads):
        at = 3 * (first_head + h)
        mark = (lane >= at) & (lane < at + 3)
        for p in range(2):
            out_p = told[p][:, h * HD : (h + 1) * HD]
            lse_p = jnp.sum(jnp.where(mark, told[p][:, wide:], 0.0), axis=1, keepdims=True)
            part = slice((2 * h + p) * half, (2 * h + p + 1) * half)
            lse_a = mine_ref[part, HD:]
            lse_b = other_ref[part, HD:]
            top = jnp.maximum(jnp.maximum(lse_a, lse_b), lse_p)
            scale_a = jnp.exp(lse_a - top)
            scale_b = jnp.exp(lse_b - top)
            scale_p = jnp.exp(lse_p - top)
            mixed = scale_a * mine_ref[part, :HD] + scale_b * other_ref[part, :HD] + scale_p * out_p
            mixed = (mixed / (scale_a + scale_b + scale_p)).astype(BF16)
            att_ref[p * half : (p + 1) * half, h * HD : (h + 1) * HD] = mixed


def merge_part(place, mine, other, own, twin, deep):
    chips, draft, _ = own.shape
    half = chips * draft
    return pl.pallas_call(
        merge_kernel,
        in_specs=[SMEM_SPEC] + [VMEM_SPEC] * 4,
        out_specs=VMEM_SPEC,
        out_shape=pltpu.VMEM((2 * half, deep), BF16),
        scratch_shapes=[
            pltpu.VMEM((half, deep + LANES), F32),
            pltpu.VMEM((half, deep + LANES), F32),
        ],
        compiler_params=pltpu.CompilerParams(vmem_limit_bytes=8 << 20),
        cost_estimate=pl.CostEstimate(
            flops=8 * mine.size, transcendentals=mine.size, bytes_accessed=0
        ),
        name="merge_part",
    )(place, on_chip(mine), on_chip(other), on_chip(own), on_chip(twin))


def project_kernel(place_ref, *refs, masks, first):
    part_ref, refs = (None, refs) if first else (refs[0], refs[1:])
    wide_ref, out_ref = refs[len(masks) :]
    total = functools.reduce(
        jnp.add,
        [
            jnp.dot(ref[...], wide_ref[place_ref[3] ^ mask], preferred_element_type=F32)
            for ref, mask in zip(refs, masks)
        ],
    )
    if first:
        out_ref[...] = total
        return
    total = total + part_ref[...]
    owners, draft, _ = out_ref.shape
    for s in range(owners):
        at = ((s % 2) * (owners // 2) + s // 2) * draft
        out_ref[s] = total[at : at + draft].astype(BF16)


def project(place, part, chunks, wide):
    masks = tuple(chunks)
    rows, deep = chunks[masks[0]].shape
    owners, _, cols = wide.shape
    first = part is None
    arrays = ([] if first else [part]) + [chunks[mask] for mask in masks] + [wide]
    shape = (rows, cols) if first else (owners, rows // owners, cols)
    return pl.pallas_call(
        functools.partial(project_kernel, masks=masks, first=first),
        in_specs=[SMEM_SPEC] + [VMEM_SPEC] * len(arrays),
        out_specs=VMEM_SPEC,
        out_shape=pltpu.VMEM(shape, F32 if first else BF16),
        compiler_params=pltpu.CompilerParams(vmem_limit_bytes=8 << 20),
        cost_estimate=pl.CostEstimate(
            flops=2 * rows * deep * len(masks) * cols, transcendentals=0, bytes_accessed=0
        ),
        name="project_first" if first else "project_last",
    )(place, *[on_chip(array) for array in arrays])


def shards(
    queries,
    draft_keys,
    draft_values,
    parents,
    private_keys,
    private_values,
    priv_lengths,
    prefix_keys,
    prefix_values,
    out_weight,
):
    own_rows = queries.shape[0]
    seq = lax.axis_size("seq")
    chips = seq // 2
    blocks = seq // KVH
    device = lax.axis_index("seq")
    rank = device % blocks
    top_bit = blocks.bit_length() - 2
    place = jnp.stack([(rank >> top_bit) & 1, device % 2, rank, device]).astype(jnp.int32)
    members = [list(range(c, seq, 2)) for c in range(2)]

    def from_partner(array, bit):
        return lax.ppermute(array, "seq", [(i, i ^ 1 << bit) for i in range(seq)])

    def among_members(array):
        return lax.all_to_all(
            array, "seq", split_axis=0, concat_axis=0, axis_index_groups=members, tiled=True
        )

    message = private_part(
        parents,
        priv_lengths,
        queries,
        draft_keys,
        draft_values,
        in_hbm(private_keys),
        in_hbm(private_values),
        blocks // 2,
        KVH // 2,
    )
    own = among_members(message)
    twin = from_partner(own, 0)

    span = min(4096, prefix_keys.shape[1])
    weight = out_weight.reshape(seq, -1, out_weight.shape[1])
    mine, gone, wide = prefix_part(place, own, twin, prefix_keys, prefix_values, weight, span)
    other = from_partner(gone, top_bit)
    for level in range(top_bit - 1, -1, -1):
        held = join(mine, other)
        half = held.shape[0] // 2
        at = (rank >> level) & 1
        mine = lax.dynamic_slice_in_dim(held, at * half, half, 0)
        other = from_partner(lax.dynamic_slice_in_dim(held, (1 - at) * half, half, 0), level)

    chunks = {0: merge_part(place, mine, other, own, twin, weight.shape[1])}

    def move(mask, source):
        chunks[mask] = lax.ppermute(
            chunks[source], "seq", [(i, i ^ mask ^ source) for i in range(seq)]
        )

    far = [4 * k for k in range(1, chips // 2)]
    for mask in [2] + far:
        move(mask, 0)
    for mask in far:
        move(mask + 2, mask)
    for mask in list(chunks):
        move(mask + 1, mask)
    late = (far[-1] + 2, far[-1] + 3)
    part = project(place, None, {m: chunks[m] for m in chunks if m not in late}, wide)
    pieces = project(place, part, {m: chunks[m] for m in late}, wide)
    done = lax.all_to_all(pieces, "seq", split_axis=0, concat_axis=0, tiled=True)
    return done.transpose(1, 0, 2).reshape(own_rows, -1).astype(F32)


def solution(mesh):
    in_specs = (
        P(("groups", "seq"), None),
        P(("groups", "seq"), None),
        P(("groups", "seq"), None),
        P(("groups", "seq")),
        P(("groups", "seq"), None, None),
        P(("groups", "seq"), None, None),
        P(("groups", "seq")),
        P(("groups", "seq"), None, None),
        P(("groups", "seq"), None, None),
        P(None, "seq"),
    )
    out_specs = P(("groups", "seq"), None)

    return jax.shard_map(shards, mesh=mesh, in_specs=in_specs, out_specs=out_specs, check_vma=False)
```

```python
import functools

import jax
import jax.numpy as jnp
from jax import lax
from jax.experimental import pallas as pl
from jax.experimental.pallas import tpu as pltpu
from jax.sharding import PartitionSpec as P


HEADS = 64
KVH = 8
HD = 128
GROUP = HEADS // KVH
SCALE = HD ** (-0.5)
LOG2E = 1.4426950408889634
LANES = 128
NEG = -1e30
LIMIT = 2.0**100
WIDE = GROUP * HD
MESSAGE = 3 * WIDE + LANES
NT = (((1,), (1,)), ((), ()))
TN = (((0,), (0,)), ((), ()))
F32 = jnp.float32
BF16 = jnp.bfloat16


def in_hbm(array):
    return pltpu.with_memory_space_constraint(array, pltpu.HBM)


def on_chip(array):
    return pltpu.with_memory_space_constraint(array, pltpu.VMEM)


VMEM_SPEC = pl.BlockSpec(memory_space=pltpu.VMEM)
SMEM_SPEC = pl.BlockSpec(memory_space=pltpu.SMEM)


def private_kernel(
    place_ref, par_ref, len_ref, q_ref, dk_ref, dv_ref, k_ref, v_ref, out_ref, *, draft, copies, batch
):
    rows = GROUP * draft
    slots = k_ref.shape[1]
    seen = []
    for i in range(draft):
        bits = jnp.int32(1 << i)
        for j in range(i):
            bits = bits | jnp.where(par_ref[i] == j, seen[j], 0)
        seen.append(bits)
    row = lax.broadcasted_iota(jnp.int32, (rows, LANES), 0) % draft
    lane = lax.broadcasted_iota(jnp.int32, (rows, LANES), 1)
    mask = jnp.zeros((rows, LANES), jnp.int32)
    for i in range(draft):
        mask = jnp.where(row == i, seen[i], mask)
    shown = (lane < draft) & ((lax.shift_right_logical(mask, jnp.minimum(lane, 31)) & 1) == 1)
    live = lax.broadcasted_iota(jnp.int32, (rows, slots), 1) < len_ref[0]
    fill = jnp.zeros((LANES - draft, HD), F32)
    stat_lane = lax.broadcasted_iota(jnp.int32, (draft, LANES), 1)
    groups = range(batch)
    queries = []
    for g in groups:
        q = q_ref[:, g * WIDE : (g + 1) * WIDE]
        for copy in range(copies):
            out_ref[g * copies + copy, :, :WIDE] = q
        q32 = q.astype(F32)
        queries.append(
            jnp.concatenate([q32[:, h * HD : (h + 1) * HD] for h in range(GROUP)], axis=0).astype(BF16)
        )
    cols = [slice(g * HD, (g + 1) * HD) for g in groups]
    scores = [
        lax.dot_general(queries[g], k_ref[0, :, cols[g]], NT, preferred_element_type=F32) for g in groups
    ]
    trees = []
    for g in groups:
        dkey = jnp.concatenate([dk_ref[:, cols[g]].astype(F32), fill], axis=0).astype(BF16)
        trees.append(lax.dot_general(queries[g], dkey, NT, preferred_element_type=F32))
    for g in groups:
        score = jnp.where(live, scores[g] * SCALE, NEG)
        tree = jnp.where(shown, trees[g] * SCALE, NEG)
        tiles = [score[:, j : j + LANES] for j in range(0, slots, LANES)] + [tree]
        peak = jnp.max(functools.reduce(jnp.maximum, tiles), axis=1, keepdims=True)
        tiles = [jnp.exp(tile - peak) for tile in tiles]
        denom = jnp.sum(functools.reduce(jnp.add, tiles), axis=1, keepdims=True)
        weights = jnp.concatenate([tile.astype(BF16) for tile in tiles[:-1]], axis=1)
        dval = jnp.concatenate([dv_ref[:, cols[g]].astype(F32), fill], axis=0).astype(BF16)
        mixture = jnp.dot(weights, v_ref[0, :, cols[g]], preferred_element_type=F32)
        mixture = mixture + jnp.dot(tiles[-1].astype(BF16), dval, preferred_element_type=F32)
        mixture = mixture / denom
        coarse = mixture.astype(BF16).astype(F32)
        fine = mixture - coarse
        lse = peak + jnp.log(denom)
        first = lse.astype(BF16).astype(F32)
        second = (lse - first).astype(BF16).astype(F32)
        third = lse - first - second
        stats = jnp.zeros((draft, LANES), F32)
        for copy in range(copies):
            at = g * copies + copy
            for h in range(GROUP):
                part = slice(h * draft, (h + 1) * draft)
                out_ref[at, :, WIDE + h * HD : WIDE + (h + 1) * HD] = coarse[part].astype(BF16)
                out_ref[at, :, 2 * WIDE + h * HD : 2 * WIDE + (h + 1) * HD] = fine[part].astype(BF16)
                if copy == 0:
                    for t, term in enumerate((first, second, third)):
                        stats = jnp.where(stat_lane == 3 * h + t, term[part], stats)
            out_ref[at, :, 3 * WIDE :] = stats.astype(BF16)


def private_part(place, parents, lengths, queries, dkeys, dvals, pkeys, pvals, copies, batch):
    draft = queries.shape[0]
    slots = pkeys.shape[1]
    return pl.pallas_call(
        functools.partial(private_kernel, draft=draft, copies=copies, batch=batch),
        grid=(KVH // batch,),
        in_specs=[
            SMEM_SPEC,
            SMEM_SPEC,
            SMEM_SPEC,
            pl.BlockSpec((draft, batch * WIDE), lambda g: (0, g)),
            pl.BlockSpec((draft, batch * HD), lambda g: (0, g)),
            pl.BlockSpec((draft, batch * HD), lambda g: (0, g)),
            pl.BlockSpec((1, slots, batch * HD), lambda g: (0, 0, g)),
            pl.BlockSpec((1, slots, batch * HD), lambda g: (0, 0, g)),
        ],
        out_specs=pl.BlockSpec((batch * copies, draft, MESSAGE), lambda g: (g, 0, 0)),
        out_shape=jax.ShapeDtypeStruct((KVH * copies, draft, MESSAGE), BF16),
        compiler_params=pltpu.CompilerParams(vmem_limit_bytes=20 << 20),
        cost_estimate=pl.CostEstimate(
            flops=4 * draft * HEADS * slots * HD,
            transcendentals=draft * HEADS * slots,
            bytes_accessed=4 * slots * KVH * HD,
        ),
        name="private_part",
    )(place, parents, lengths, queries, dkeys, dvals, pkeys, pvals)


def prefix_kernel(
    place_ref,
    told_ref,
    k_ref,
    v_ref,
    twin_k_ref,
    twin_v_ref,
    w_ref,
    out_ref,
    wide_ref,
    told32,
    qs,
    peak,
    denom,
    acc,
    sem,
):
    step = pl.program_id(0)
    chips, draft, _ = told_ref.shape
    owned = chips * draft
    rows = owned * GROUP
    span = k_ref.shape[1]
    fetch = pltpu.make_async_copy(w_ref, wide_ref, sem)

    @pl.when(step == 2)
    def _():
        fetch.start()

    @pl.when(step == 0)
    def _():
        for j in range(chips):
            told32[j * draft : (j + 1) * draft, :] = told_ref[j, :, :WIDE].astype(F32)
        for h in range(GROUP):
            qs[h * owned : (h + 1) * owned, :] = told32[:, h * HD : (h + 1) * HD].astype(BF16)
        head = lax.dot_general(k_ref[0, :HD, :], qs[...], NT, preferred_element_type=F32)
        peak[...] = jnp.max(head, axis=0, keepdims=True) * (SCALE * LOG2E)
        denom[...] = jnp.zeros(denom.shape, F32)
        acc[...] = jnp.zeros(acc.shape, F32)

    keys = (k_ref[0], twin_k_ref[0])
    values = (v_ref[0], twin_v_ref[0])
    scores = [lax.dot_general(key, qs[...], NT, preferred_element_type=F32) for key in keys]
    weights = [jnp.exp2(score * (SCALE * LOG2E) - peak[...]) for score in scores]
    sums = [jnp.sum(weight.reshape(span // 8, 8, rows), axis=0) for weight in weights]
    mixes = [
        lax.dot_general(value, weight.astype(BF16), TN, preferred_element_type=F32)
        for value, weight in zip(values, weights)
    ]
    sums = [denom[i] + sums[i] for i in range(2)]
    mixes = [acc[i] + mixes[i] for i in range(2)]
    fits = jnp.max(jnp.maximum(sums[0], sums[1])) < LIMIT

    @pl.when(fits)
    def _():
        for i in range(2):
            denom[i] = sums[i]
            acc[i] = mixes[i]

    @pl.when(jnp.logical_not(fits))
    def _():
        part = 4 * HD

        def careful(i, keys, values):
            scores = lax.dot_general(keys, qs[...], NT, preferred_element_type=F32)
            scores = scores * (SCALE * LOG2E)
            old = peak[...]
            new = jnp.maximum(old, jnp.max(scores, axis=0, keepdims=True))
            fade = jnp.exp2(old - new)
            weights = jnp.exp2(scores - new)
            peak[...] = new
            sums = jnp.sum(weights.reshape(part // 8, 8, rows), axis=0)
            mixes = lax.dot_general(values, weights.astype(BF16), TN, preferred_element_type=F32)
            denom[i] = denom[i] * fade + sums
            acc[i] = acc[i] * fade + mixes
            denom[1 - i] = denom[1 - i] * fade
            acc[1 - i] = acc[1 - i] * fade

        @pl.loop(0, span // part)
        def _(b):
            block = pl.ds(pl.multiple_of(b * part, part), part)
            careful(0, k_ref[0, block, :], v_ref[0, block, :])
            careful(1, twin_k_ref[0, block, :], twin_v_ref[0, block, :])

    @pl.when(step == pl.num_programs(0) - 1)
    def _():
        total = jnp.sum(denom[0] + denom[1], axis=0, keepdims=True)
        lse = peak[...] * (1.0 / LOG2E) + jnp.log(total)
        out_ref[:, :HD] = ((acc[0] + acc[1]) / total).T
        out_ref[:, HD:] = jnp.broadcast_to(lse, (LANES, rows)).T
        fetch.wait()


def prefix_part(place, told, keys, values, twin_keys, twin_values, weight, span):
    chips, draft, _ = told.shape
    owned = chips * draft
    rows = owned * GROUP
    return pl.pallas_call(
        prefix_kernel,
        grid=(keys.shape[1] // span,),
        in_specs=[
            SMEM_SPEC,
            pl.BlockSpec(told.shape, lambda i: (0, 0, 0)),
            pl.BlockSpec((1, span, HD), lambda i: (0, i, 0)),
            pl.BlockSpec((1, span, HD), lambda i: (0, i, 0)),
            pl.BlockSpec((1, span, HD), lambda i: (0, i, 0)),
            pl.BlockSpec((1, span, HD), lambda i: (0, i, 0)),
            pl.BlockSpec(memory_space=pl.ANY),
        ],
        out_specs=[pl.BlockSpec((rows, HD + LANES), lambda i: (0, 0)), VMEM_SPEC],
        out_shape=[
            jax.ShapeDtypeStruct((rows, HD + LANES), F32),
            pltpu.VMEM(weight.shape, BF16),
        ],
        scratch_shapes=[
            pltpu.VMEM((owned, WIDE), F32),
            pltpu.VMEM((rows, HD), BF16),
            pltpu.VMEM((1, rows), F32),
            pltpu.VMEM((2, 8, rows), F32),
            pltpu.VMEM((2, HD, rows), F32),
            pltpu.SemaphoreType.DMA,
        ],
        compiler_params=pltpu.CompilerParams(vmem_limit_bytes=40 << 20),
        cost_estimate=pl.CostEstimate(
            flops=8 * rows * keys.shape[1] * HD,
            transcendentals=2 * rows * keys.shape[1],
            bytes_accessed=4 * keys.shape[1] * HD,
        ),
        name="prefix_part",
    )(
        place,
        on_chip(told),
        in_hbm(keys),
        in_hbm(values),
        in_hbm(twin_keys),
        in_hbm(twin_values),
        in_hbm(weight),
    )


def join(first, second):
    out_a, lse_a = first[:, :HD], first[:, HD:]
    out_b, lse_b = second[:, :HD], second[:, HD:]
    top = jnp.maximum(lse_a, lse_b)
    scale_a = jnp.exp(lse_a - top)
    scale_b = jnp.exp(lse_b - top)
    both = scale_a + scale_b
    return jnp.concatenate(
        [(scale_a * out_a + scale_b * out_b) / both, top + jnp.log(both)], axis=1
    )


def merge_kernel(place_ref, mine_ref, told_ref, att_ref, told32):
    chips, draft, _ = told_ref.shape
    owned = chips * draft
    wide = att_ref.shape[1]
    heads = wide // HD
    first_head = place_ref[2] * heads
    col = pl.multiple_of(first_head * HD, wide)
    for j in range(chips):
        part = slice(j * draft, (j + 1) * draft)
        told32[part, :wide] = told_ref[j, :, pl.ds(WIDE + col, wide)].astype(F32) + told_ref[
            j, :, pl.ds(2 * WIDE + col, wide)
        ].astype(F32)
        told32[part, wide:] = told_ref[j, :, 3 * WIDE :].astype(F32)
    stats = told32[:, wide:]
    lane = lax.broadcasted_iota(jnp.int32, (owned, LANES), 1)
    for h in range(heads):
        at = 3 * (first_head + h)
        mark = (lane >= at) & (lane < at + 3)
        lse_p = jnp.sum(jnp.where(mark, stats, 0.0), axis=1, keepdims=True)
        part = slice(h * owned, (h + 1) * owned)
        lse_a = mine_ref[part, HD:]
        top = jnp.maximum(lse_a, lse_p)
        scale_a = jnp.exp(lse_a - top)
        scale_p = jnp.exp(lse_p - top)
        mixed = scale_a * mine_ref[part, :HD] + scale_p * told32[:, h * HD : (h + 1) * HD]
        att_ref[:, h * HD : (h + 1) * HD] = (mixed / (scale_a + scale_p)).astype(BF16)


def merge_part(place, mine, told):
    chips, draft, _ = told.shape
    owned = chips * draft
    wide = mine.shape[0] // owned * HD
    return pl.pallas_call(
        merge_kernel,
        in_specs=[SMEM_SPEC, VMEM_SPEC, VMEM_SPEC],
        out_specs=VMEM_SPEC,
        out_shape=pltpu.VMEM((owned, wide), BF16),
        scratch_shapes=[pltpu.VMEM((owned, wide + LANES), F32)],
        compiler_params=pltpu.CompilerParams(vmem_limit_bytes=8 << 20),
        cost_estimate=pl.CostEstimate(
            flops=8 * mine.size, transcendentals=mine.size, bytes_accessed=0
        ),
        name="merge_part",
    )(place, on_chip(mine), on_chip(told))


def project_kernel(place_ref, *refs, masks, first):
    part_ref, refs = (None, refs) if first else (refs[0], refs[1:])
    wide_ref, out_ref = refs[2 * len(masks) :]
    chip = place_ref[0]
    total = functools.reduce(
        jnp.add,
        [
            jnp.dot(
                jnp.concatenate([refs[2 * i][...], refs[2 * i + 1][...]], axis=0),
                wide_ref[chip ^ mask],
                preferred_element_type=F32,
            )
            for i, mask in enumerate(masks)
        ],
    )
    if first:
        out_ref[...] = total
        return
    total = total + part_ref[...]
    owners, draft, _ = out_ref.shape
    half = owners // 2 * draft
    own, twin = total[:half], total[half:]
    even = place_ref[1] == 0
    halves = (jnp.where(even, own, twin), jnp.where(even, twin, own))
    for s in range(owners):
        at = s // 2 * draft
        out_ref[s] = halves[s % 2][at : at + draft].astype(BF16)


def project(place, part, chunks, wide, owners):
    masks = tuple(chunks)
    rows, deep = chunks[masks[0]][0].shape
    cols = wide.shape[2]
    first = part is None
    arrays = [] if first else [part]
    for mask in masks:
        arrays.extend(chunks[mask])
    arrays.append(wide)
    shape = (2 * rows, cols) if first else (owners, 2 * rows // owners, cols)
    return pl.pallas_call(
        functools.partial(project_kernel, masks=masks, first=first),
        in_specs=[SMEM_SPEC] + [VMEM_SPEC] * len(arrays),
        out_specs=VMEM_SPEC,
        out_shape=pltpu.VMEM(shape, F32 if first else BF16),
        compiler_params=pltpu.CompilerParams(vmem_limit_bytes=8 << 20),
        cost_estimate=pl.CostEstimate(
            flops=4 * rows * deep * len(masks) * cols, transcendentals=0, bytes_accessed=0
        ),
        name="project_first" if first else "project_last",
    )(place, *[on_chip(array) for array in arrays])


def shards(
    queries,
    draft_keys,
    draft_values,
    parents,
    private_keys,
    private_values,
    priv_lengths,
    prefix_keys,
    prefix_values,
    out_weight,
):
    own_rows = queries.shape[0]
    seq = lax.axis_size("seq")
    chips = seq // 2
    blocks = seq // KVH
    device = lax.axis_index("seq")
    chip = device // 2
    sharers = blocks // 2
    rank = chip % sharers
    place = jnp.stack([chip, device % 2, rank]).astype(jnp.int32)
    members = [list(range(c, seq, 2)) for c in range(2)]

    def from_partner(array, mask):
        return lax.ppermute(array, "seq", [(i, i ^ mask) for i in range(seq)])

    twin_keys = from_partner(prefix_keys, 1)
    twin_values = from_partner(prefix_values, 1)
    message = private_part(
        place,
        in_hbm(parents),
        priv_lengths,
        in_hbm(queries),
        in_hbm(draft_keys),
        in_hbm(draft_values),
        in_hbm(private_keys),
        in_hbm(private_values),
        sharers,
        KVH // 2,
    )
    told = lax.all_to_all(
        message, "seq", split_axis=0, concat_axis=0, axis_index_groups=members, tiled=True
    )

    span = min(4096, prefix_keys.shape[1])
    weight = out_weight.reshape(chips, -1, out_weight.shape[1])
    mine, wide = prefix_part(
        place, told, prefix_keys, prefix_values, twin_keys, twin_values, weight, span
    )
    for level in range(sharers.bit_length() - 2, -1, -1):
        half = mine.shape[0] // 2
        at = (rank >> level) & 1
        kept = lax.dynamic_slice_in_dim(mine, at * half, half, 0)
        gone = lax.dynamic_slice_in_dim(mine, (1 - at) * half, half, 0)
        mine = join(kept, from_partner(gone, 2 << level))

    own = {0: merge_part(place, mine, told)}
    twin = {}
    far = [2 * k for k in range(1, chips // 2)]
    for mask in [1] + far:
        own[mask] = from_partner(own[0], 2 * mask)
    for mask in far:
        own[mask + 1] = from_partner(own[mask], 2)
    for mask in own:
        twin[mask] = from_partner(own[mask], 1)
    both = {mask: (own[mask], twin[mask]) for mask in own}
    last = far[-1] + 1
    early = {mask: both[mask] for mask in both if mask != last}
    part = project(place, None, early, wide, seq)
    pieces = project(place, part, {last: both[last]}, wide, seq)
    done = lax.all_to_all(pieces, "seq", split_axis=0, concat_axis=0, tiled=True)
    return done.transpose(1, 0, 2).reshape(own_rows, -1).astype(F32)


def solution(mesh):
    in_specs = (
        P(("groups", "seq"), None),
        P(("groups", "seq"), None),
        P(("groups", "seq"), None),
        P(("groups", "seq")),
        P(("groups", "seq"), None, None),
        P(("groups", "seq"), None, None),
        P(("groups", "seq")),
        P(("groups", "seq"), None, None),
        P(("groups", "seq"), None, None),
        P(None, "seq"),
    )
    out_specs = P(("groups", "seq"), None)

    return jax.shard_map(shards, mesh=mesh, in_specs=in_specs, out_specs=out_specs, check_vma=False)
```

```python
import functools

import jax
import jax.numpy as jnp
from jax import lax
from jax.experimental import pallas as pl
from jax.experimental.pallas import tpu as pltpu
from jax.sharding import PartitionSpec as P


HEADS = 64
KVH = 8
HD = 128
GROUP = HEADS // KVH
SCALE = HD ** (-0.5)
LOG2E = 1.4426950408889634
LANES = 128
NEG = -1e30
LIMIT = 2.0**100
WIDE = GROUP * HD
MESSAGE = 3 * WIDE + LANES
NT = (((1,), (1,)), ((), ()))
TN = (((0,), (0,)), ((), ()))
F32 = jnp.float32
BF16 = jnp.bfloat16


def in_hbm(array):
    return pltpu.with_memory_space_constraint(array, pltpu.HBM)


def on_chip(array):
    return pltpu.with_memory_space_constraint(array, pltpu.VMEM)


VMEM_SPEC = pl.BlockSpec(memory_space=pltpu.VMEM)
SMEM_SPEC = pl.BlockSpec(memory_space=pltpu.SMEM)


def private_kernel(
    place_ref, par_ref, len_ref, q_ref, dk_ref, dv_ref, k_ref, v_ref, out_ref, *, draft, copies, batch
):
    rows = GROUP * draft
    slots = k_ref.shape[1]
    seen = []
    for i in range(draft):
        bits = jnp.int32(1 << i)
        for j in range(i):
            bits = bits | jnp.where(par_ref[i] == j, seen[j], 0)
        seen.append(bits)
    row = lax.broadcasted_iota(jnp.int32, (rows, LANES), 0) % draft
    lane = lax.broadcasted_iota(jnp.int32, (rows, LANES), 1)
    mask = jnp.zeros((rows, LANES), jnp.int32)
    for i in range(draft):
        mask = jnp.where(row == i, seen[i], mask)
    shown = (lane < draft) & ((lax.shift_right_logical(mask, jnp.minimum(lane, 31)) & 1) == 1)
    live = lax.broadcasted_iota(jnp.int32, (rows, slots), 1) < len_ref[0]
    fill = jnp.zeros((LANES - draft, HD), F32)
    stat_lane = lax.broadcasted_iota(jnp.int32, (draft, LANES), 1)
    groups = range(batch)
    queries = []
    for g in groups:
        q = q_ref[:, g * WIDE : (g + 1) * WIDE]
        for copy in range(copies):
            out_ref[g * copies + copy, :, :WIDE] = q
        q32 = q.astype(F32)
        queries.append(
            jnp.concatenate([q32[:, h * HD : (h + 1) * HD] for h in range(GROUP)], axis=0).astype(BF16)
        )
    cols = [slice(g * HD, (g + 1) * HD) for g in groups]
    scores = [
        lax.dot_general(queries[g], k_ref[0, :, cols[g]], NT, preferred_element_type=F32) for g in groups
    ]
    trees = []
    for g in groups:
        dkey = jnp.concatenate([dk_ref[:, cols[g]].astype(F32), fill], axis=0).astype(BF16)
        trees.append(lax.dot_general(queries[g], dkey, NT, preferred_element_type=F32))
    for g in groups:
        score = jnp.where(live, scores[g] * SCALE, NEG)
        tree = jnp.where(shown, trees[g] * SCALE, NEG)
        tiles = [score[:, j : j + LANES] for j in range(0, slots, LANES)] + [tree]
        peak = jnp.max(functools.reduce(jnp.maximum, tiles), axis=1, keepdims=True)
        tiles = [jnp.exp(tile - peak) for tile in tiles]
        denom = jnp.sum(functools.reduce(jnp.add, tiles), axis=1, keepdims=True)
        weights = jnp.concatenate([tile.astype(BF16) for tile in tiles[:-1]], axis=1)
        dval = jnp.concatenate([dv_ref[:, cols[g]].astype(F32), fill], axis=0).astype(BF16)
        mixture = jnp.dot(weights, v_ref[0, :, cols[g]], preferred_element_type=F32)
        mixture = mixture + jnp.dot(tiles[-1].astype(BF16), dval, preferred_element_type=F32)
        mixture = mixture / denom
        coarse = mixture.astype(BF16).astype(F32)
        fine = mixture - coarse
        lse = peak + jnp.log(denom)
        first = lse.astype(BF16).astype(F32)
        second = (lse - first).astype(BF16).astype(F32)
        third = lse - first - second
        stats = jnp.zeros((draft, LANES), F32)
        for copy in range(copies):
            at = g * copies + copy
            for h in range(GROUP):
                part = slice(h * draft, (h + 1) * draft)
                out_ref[at, :, WIDE + h * HD : WIDE + (h + 1) * HD] = coarse[part].astype(BF16)
                out_ref[at, :, 2 * WIDE + h * HD : 2 * WIDE + (h + 1) * HD] = fine[part].astype(BF16)
                if copy == 0:
                    for t, term in enumerate((first, second, third)):
                        stats = jnp.where(stat_lane == 3 * h + t, term[part], stats)
            out_ref[at, :, 3 * WIDE :] = stats.astype(BF16)


def private_part(place, parents, lengths, queries, dkeys, dvals, pkeys, pvals, copies, batch):
    draft = queries.shape[0]
    slots = pkeys.shape[1]
    return pl.pallas_call(
        functools.partial(private_kernel, draft=draft, copies=copies, batch=batch),
        grid=(KVH // batch,),
        in_specs=[
            SMEM_SPEC,
            SMEM_SPEC,
            SMEM_SPEC,
            pl.BlockSpec((draft, batch * WIDE), lambda g: (0, g)),
            pl.BlockSpec((draft, batch * HD), lambda g: (0, g)),
            pl.BlockSpec((draft, batch * HD), lambda g: (0, g)),
            pl.BlockSpec((1, slots, batch * HD), lambda g: (0, 0, g)),
            pl.BlockSpec((1, slots, batch * HD), lambda g: (0, 0, g)),
        ],
        out_specs=pl.BlockSpec((batch * copies, draft, MESSAGE), lambda g: (g, 0, 0)),
        out_shape=jax.ShapeDtypeStruct((KVH * copies, draft, MESSAGE), BF16),
        compiler_params=pltpu.CompilerParams(vmem_limit_bytes=20 << 20),
        cost_estimate=pl.CostEstimate(
            flops=4 * draft * HEADS * slots * HD,
            transcendentals=draft * HEADS * slots,
            bytes_accessed=4 * slots * KVH * HD,
        ),
        name="private_part",
    )(place, parents, lengths, queries, dkeys, dvals, pkeys, pvals)


def prefix_kernel(
    place_ref,
    told_ref,
    k_ref,
    v_ref,
    twin_k_ref,
    twin_v_ref,
    w_ref,
    out_ref,
    wide_ref,
    told32,
    qs,
    peak,
    denom,
    acc,
    sem,
):
    step = pl.program_id(0)
    chips, draft, _ = told_ref.shape
    owned = chips * draft
    rows = owned * GROUP
    span = k_ref.shape[1]
    fetch = pltpu.make_async_copy(w_ref, wide_ref, sem)

    @pl.when(step == 2)
    def _():
        fetch.start()

    @pl.when(step == 0)
    def _():
        for j in range(chips):
            told32[j * draft : (j + 1) * draft, :] = told_ref[j, :, :WIDE].astype(F32)
        for h in range(GROUP):
            qs[h * owned : (h + 1) * owned, :] = told32[:, h * HD : (h + 1) * HD].astype(BF16)
        head = lax.dot_general(k_ref[0, :HD, :], qs[...], NT, preferred_element_type=F32)
        peak[...] = jnp.max(head, axis=0, keepdims=True) * (SCALE * LOG2E)
        denom[...] = jnp.zeros(denom.shape, F32)
        acc[...] = jnp.zeros(acc.shape, F32)

    keys = (k_ref[0], twin_k_ref[0])
    values = (v_ref[0], twin_v_ref[0])
    scores = [lax.dot_general(key, qs[...], NT, preferred_element_type=F32) for key in keys]
    weights = [jnp.exp2(score * (SCALE * LOG2E) - peak[...]) for score in scores]
    sums = [jnp.sum(weight.reshape(span // 8, 8, rows), axis=0) for weight in weights]
    mixes = [
        lax.dot_general(value, weight.astype(BF16), TN, preferred_element_type=F32)
        for value, weight in zip(values, weights)
    ]
    sums = [denom[i] + sums[i] for i in range(2)]
    mixes = [acc[i] + mixes[i] for i in range(2)]
    fits = jnp.max(jnp.maximum(sums[0], sums[1])) < LIMIT

    @pl.when(fits)
    def _():
        for i in range(2):
            denom[i] = sums[i]
            acc[i] = mixes[i]

    @pl.when(jnp.logical_not(fits))
    def _():
        part = 4 * HD

        def careful(i, keys, values):
            scores = lax.dot_general(keys, qs[...], NT, preferred_element_type=F32)
            scores = scores * (SCALE * LOG2E)
            old = peak[...]
            new = jnp.maximum(old, jnp.max(scores, axis=0, keepdims=True))
            fade = jnp.exp2(old - new)
            weights = jnp.exp2(scores - new)
            peak[...] = new
            sums = jnp.sum(weights.reshape(part // 8, 8, rows), axis=0)
            mixes = lax.dot_general(values, weights.astype(BF16), TN, preferred_element_type=F32)
            denom[i] = denom[i] * fade + sums
            acc[i] = acc[i] * fade + mixes
            denom[1 - i] = denom[1 - i] * fade
            acc[1 - i] = acc[1 - i] * fade

        @pl.loop(0, span // part)
        def _(b):
            block = pl.ds(pl.multiple_of(b * part, part), part)
            careful(0, k_ref[0, block, :], v_ref[0, block, :])
            careful(1, twin_k_ref[0, block, :], twin_v_ref[0, block, :])

    @pl.when(step == pl.num_programs(0) - 1)
    def _():
        total = jnp.sum(denom[0] + denom[1], axis=0, keepdims=True)
        lse = peak[...] * (1.0 / LOG2E) + jnp.log(total)
        out_ref[:, :HD] = ((acc[0] + acc[1]) / total).T
        out_ref[:, HD:] = jnp.broadcast_to(lse, (LANES, rows)).T
        fetch.wait()


def prefix_part(place, told, keys, values, twin_keys, twin_values, weight, span):
    chips, draft, _ = told.shape
    owned = chips * draft
    rows = owned * GROUP
    return pl.pallas_call(
        prefix_kernel,
        grid=(keys.shape[1] // span,),
        in_specs=[
            SMEM_SPEC,
            pl.BlockSpec(told.shape, lambda i: (0, 0, 0)),
            pl.BlockSpec((1, span, HD), lambda i: (0, i, 0)),
            pl.BlockSpec((1, span, HD), lambda i: (0, i, 0)),
            pl.BlockSpec((1, span, HD), lambda i: (0, i, 0)),
            pl.BlockSpec((1, span, HD), lambda i: (0, i, 0)),
            pl.BlockSpec(memory_space=pl.ANY),
        ],
        out_specs=[pl.BlockSpec((rows, HD + LANES), lambda i: (0, 0)), VMEM_SPEC],
        out_shape=[
            jax.ShapeDtypeStruct((rows, HD + LANES), F32),
            pltpu.VMEM(weight.shape, BF16),
        ],
        scratch_shapes=[
            pltpu.VMEM((owned, WIDE), F32),
            pltpu.VMEM((rows, HD), BF16),
            pltpu.VMEM((1, rows), F32),
            pltpu.VMEM((2, 8, rows), F32),
            pltpu.VMEM((2, HD, rows), F32),
            pltpu.SemaphoreType.DMA,
        ],
        compiler_params=pltpu.CompilerParams(vmem_limit_bytes=40 << 20),
        cost_estimate=pl.CostEstimate(
            flops=8 * rows * keys.shape[1] * HD,
            transcendentals=2 * rows * keys.shape[1],
            bytes_accessed=4 * keys.shape[1] * HD,
        ),
        name="prefix_part",
    )(
        place,
        on_chip(told),
        in_hbm(keys),
        in_hbm(values),
        in_hbm(twin_keys),
        in_hbm(twin_values),
        in_hbm(weight),
    )


def join(first, second):
    out_a, lse_a = first[:, :HD], first[:, HD:]
    out_b, lse_b = second[:, :HD], second[:, HD:]
    top = jnp.maximum(lse_a, lse_b)
    scale_a = jnp.exp(lse_a - top)
    scale_b = jnp.exp(lse_b - top)
    both = scale_a + scale_b
    return jnp.concatenate(
        [(scale_a * out_a + scale_b * out_b) / both, top + jnp.log(both)], axis=1
    )


def merge_kernel(place_ref, mine_ref, told_ref, att_ref, told32):
    chips, draft, _ = told_ref.shape
    owned = chips * draft
    wide = att_ref.shape[1]
    heads = wide // HD
    first_head = place_ref[2] * heads
    col = pl.multiple_of(first_head * HD, wide)
    for j in range(chips):
        part = slice(j * draft, (j + 1) * draft)
        told32[part, :wide] = told_ref[j, :, pl.ds(WIDE + col, wide)].astype(F32) + told_ref[
            j, :, pl.ds(2 * WIDE + col, wide)
        ].astype(F32)
        told32[part, wide:] = told_ref[j, :, 3 * WIDE :].astype(F32)
    stats = told32[:, wide:]
    lane = lax.broadcasted_iota(jnp.int32, (owned, LANES), 1)
    for h in range(heads):
        at = 3 * (first_head + h)
        mark = (lane >= at) & (lane < at + 3)
        lse_p = jnp.sum(jnp.where(mark, stats, 0.0), axis=1, keepdims=True)
        part = slice(h * owned, (h + 1) * owned)
        lse_a = mine_ref[part, HD:]
        top = jnp.maximum(lse_a, lse_p)
        scale_a = jnp.exp(lse_a - top)
        scale_p = jnp.exp(lse_p - top)
        mixed = scale_a * mine_ref[part, :HD] + scale_p * told32[:, h * HD : (h + 1) * HD]
        att_ref[:, h * HD : (h + 1) * HD] = (mixed / (scale_a + scale_p)).astype(BF16)


def merge_part(place, mine, told):
    chips, draft, _ = told.shape
    owned = chips * draft
    wide = mine.shape[0] // owned * HD
    return pl.pallas_call(
        merge_kernel,
        in_specs=[SMEM_SPEC, VMEM_SPEC, VMEM_SPEC],
        out_specs=VMEM_SPEC,
        out_shape=pltpu.VMEM((owned, wide), BF16),
        scratch_shapes=[pltpu.VMEM((owned, wide + LANES), F32)],
        compiler_params=pltpu.CompilerParams(vmem_limit_bytes=8 << 20),
        cost_estimate=pl.CostEstimate(
            flops=8 * mine.size, transcendentals=mine.size, bytes_accessed=0
        ),
        name="merge_part",
    )(place, on_chip(mine), on_chip(told))


def project_kernel(place_ref, *refs, masks, first, last):
    part_ref, refs = (None, refs) if first else (refs[0], refs[1:])
    wide_ref, out_ref = refs[2 * len(masks) :]
    chip = place_ref[0]
    total = functools.reduce(
        jnp.add,
        [
            jnp.dot(
                jnp.concatenate([refs[2 * i][...], refs[2 * i + 1][...]], axis=0),
                wide_ref[chip ^ mask],
                preferred_element_type=F32,
            )
            for i, mask in enumerate(masks)
        ],
    )
    if not first:
        total = total + part_ref[...]
    if not last:
        out_ref[...] = total
        return
    owners, draft, _ = out_ref.shape
    half = owners // 2 * draft
    own, twin = total[:half], total[half:]
    even = place_ref[1] == 0
    halves = (jnp.where(even, own, twin), jnp.where(even, twin, own))
    for s in range(owners):
        at = s // 2 * draft
        out_ref[s] = halves[s % 2][at : at + draft].astype(BF16)


def project(place, part, chunks, wide, owners, last):
    masks = tuple(chunks)
    rows, deep = chunks[masks[0]][0].shape
    cols = wide.shape[2]
    first = part is None
    arrays = [] if first else [part]
    for mask in masks:
        arrays.extend(chunks[mask])
    arrays.append(wide)
    shape = (owners, 2 * rows // owners, cols) if last else (2 * rows, cols)
    return pl.pallas_call(
        functools.partial(project_kernel, masks=masks, first=first, last=last),
        in_specs=[SMEM_SPEC] + [VMEM_SPEC] * len(arrays),
        out_specs=VMEM_SPEC,
        out_shape=pltpu.VMEM(shape, BF16 if last else F32),
        compiler_params=pltpu.CompilerParams(vmem_limit_bytes=8 << 20),
        cost_estimate=pl.CostEstimate(
            flops=4 * rows * deep * len(masks) * cols, transcendentals=0, bytes_accessed=0
        ),
        name="project_last" if last else "project",
    )(place, *[on_chip(array) for array in arrays])


def shards(
    queries,
    draft_keys,
    draft_values,
    parents,
    private_keys,
    private_values,
    priv_lengths,
    prefix_keys,
    prefix_values,
    out_weight,
):
    own_rows = queries.shape[0]
    seq = lax.axis_size("seq")
    chips = seq // 2
    blocks = seq // KVH
    device = lax.axis_index("seq")
    chip = device // 2
    sharers = blocks // 2
    rank = chip % sharers
    place = jnp.stack([chip, device % 2, rank]).astype(jnp.int32)
    members = [list(range(c, seq, 2)) for c in range(2)]

    def from_partner(array, mask):
        return lax.ppermute(array, "seq", [(i, i ^ mask) for i in range(seq)])

    twin_keys = from_partner(prefix_keys, 1)
    twin_values = from_partner(prefix_values, 1)
    message = private_part(
        place,
        in_hbm(parents),
        priv_lengths,
        in_hbm(queries),
        in_hbm(draft_keys),
        in_hbm(draft_values),
        in_hbm(private_keys),
        in_hbm(private_values),
        sharers,
        KVH // 2,
    )
    told = lax.all_to_all(
        message, "seq", split_axis=0, concat_axis=0, axis_index_groups=members, tiled=True
    )

    span = min(4096, prefix_keys.shape[1])
    weight = out_weight.reshape(chips, -1, out_weight.shape[1])
    mine, wide = prefix_part(
        place, told, prefix_keys, prefix_values, twin_keys, twin_values, weight, span
    )
    for level in range(sharers.bit_length() - 2, -1, -1):
        half = mine.shape[0] // 2
        at = (rank >> level) & 1
        kept = lax.dynamic_slice_in_dim(mine, at * half, half, 0)
        gone = lax.dynamic_slice_in_dim(mine, (1 - at) * half, half, 0)
        mine = join(kept, from_partner(gone, 2 << level))

    own = {0: merge_part(place, mine, told)}
    twin = {}
    far = [2 * k for k in range(1, chips // 2)]

    def move(target, mask, source, step):
        target[mask] = from_partner(source, step)

    for mask in [1] + far:
        move(own, mask, own[0], 2 * mask)
    for mask in far:
        move(own, mask + 1, own[mask], 2)
    for mask in own:
        move(twin, mask, own[mask], 1)
    stages = [[0] + far[:-1], [1, far[-1]] + [m + 1 for m in far[:-1]], [far[-1] + 1]]
    part = None
    for number, stage in enumerate(stages):
        chunks = {mask: (own[mask], twin[mask]) for mask in stage}
        part = project(place, part, chunks, wide, seq, number == len(stages) - 1)
    pieces = part
    done = lax.all_to_all(pieces, "seq", split_axis=0, concat_axis=0, tiled=True)
    return done.transpose(1, 0, 2).reshape(own_rows, -1).astype(F32)


def solution(mesh):
    in_specs = (
        P(("groups", "seq"), None),
        P(("groups", "seq"), None),
        P(("groups", "seq"), None),
        P(("groups", "seq")),
        P(("groups", "seq"), None, None),
        P(("groups", "seq"), None, None),
        P(("groups", "seq")),
        P(("groups", "seq"), None, None),
        P(("groups", "seq"), None, None),
        P(None, "seq"),
    )
    out_specs = P(("groups", "seq"), None)

    return jax.shard_map(shards, mesh=mesh, in_specs=in_specs, out_specs=out_specs, check_vma=False)
```

```python
import functools

import jax
import jax.numpy as jnp
from jax import lax
from jax.experimental import pallas as pl
from jax.experimental.pallas import tpu as pltpu
from jax.sharding import PartitionSpec as P


HEADS = 64
KVH = 8
HD = 128
GROUP = HEADS // KVH
SCALE = HD ** (-0.5)
LOG2E = 1.4426950408889634
LANES = 128
NEG = -1e30
LIMIT = 2.0**100
WIDE = GROUP * HD
MESSAGE = 3 * WIDE + LANES
NT = (((1,), (1,)), ((), ()))
TN = (((0,), (0,)), ((), ()))
F32 = jnp.float32
BF16 = jnp.bfloat16


def in_hbm(array):
    return pltpu.with_memory_space_constraint(array, pltpu.HBM)


def on_chip(array):
    return pltpu.with_memory_space_constraint(array, pltpu.VMEM)


VMEM_SPEC = pl.BlockSpec(memory_space=pltpu.VMEM)
SMEM_SPEC = pl.BlockSpec(memory_space=pltpu.SMEM)


def private_kernel(
    place_ref, par_ref, len_ref, q_ref, dk_ref, dv_ref, k_ref, v_ref, out_ref, *, draft, copies, batch
):
    rows = GROUP * draft
    slots = k_ref.shape[1]
    seen = []
    for i in range(draft):
        bits = jnp.int32(1 << i)
        for j in range(i):
            bits = bits | jnp.where(par_ref[i] == j, seen[j], 0)
        seen.append(bits)
    row = lax.broadcasted_iota(jnp.int32, (rows, LANES), 0) % draft
    lane = lax.broadcasted_iota(jnp.int32, (rows, LANES), 1)
    mask = jnp.zeros((rows, LANES), jnp.int32)
    for i in range(draft):
        mask = jnp.where(row == i, seen[i], mask)
    shown = (lane < draft) & ((lax.shift_right_logical(mask, jnp.minimum(lane, 31)) & 1) == 1)
    live = lax.broadcasted_iota(jnp.int32, (rows, slots), 1) < len_ref[0]
    fill = jnp.zeros((LANES - draft, HD), F32)
    stat_lane = lax.broadcasted_iota(jnp.int32, (draft, LANES), 1)
    groups = range(batch)
    queries = []
    for g in groups:
        q = q_ref[:, g * WIDE : (g + 1) * WIDE]
        for copy in range(copies):
            out_ref[g * copies + copy, :, :WIDE] = q
        q32 = q.astype(F32)
        queries.append(
            jnp.concatenate([q32[:, h * HD : (h + 1) * HD] for h in range(GROUP)], axis=0).astype(BF16)
        )
    cols = [slice(g * HD, (g + 1) * HD) for g in groups]
    scores = [
        lax.dot_general(queries[g], k_ref[0, :, cols[g]], NT, preferred_element_type=F32) for g in groups
    ]
    trees = []
    for g in groups:
        dkey = jnp.concatenate([dk_ref[:, cols[g]].astype(F32), fill], axis=0).astype(BF16)
        trees.append(lax.dot_general(queries[g], dkey, NT, preferred_element_type=F32))
    for g in groups:
        score = jnp.where(live, scores[g] * SCALE, NEG)
        tree = jnp.where(shown, trees[g] * SCALE, NEG)
        tiles = [score[:, j : j + LANES] for j in range(0, slots, LANES)] + [tree]
        peak = jnp.max(functools.reduce(jnp.maximum, tiles), axis=1, keepdims=True)
        tiles = [jnp.exp(tile - peak) for tile in tiles]
        denom = jnp.sum(functools.reduce(jnp.add, tiles), axis=1, keepdims=True)
        weights = jnp.concatenate([tile.astype(BF16) for tile in tiles[:-1]], axis=1)
        dval = jnp.concatenate([dv_ref[:, cols[g]].astype(F32), fill], axis=0).astype(BF16)
        mixture = jnp.dot(weights, v_ref[0, :, cols[g]], preferred_element_type=F32)
        mixture = mixture + jnp.dot(tiles[-1].astype(BF16), dval, preferred_element_type=F32)
        mixture = mixture / denom
        coarse = mixture.astype(BF16).astype(F32)
        fine = mixture - coarse
        lse = peak + jnp.log(denom)
        first = lse.astype(BF16).astype(F32)
        second = (lse - first).astype(BF16).astype(F32)
        third = lse - first - second
        stats = jnp.zeros((draft, LANES), F32)
        for copy in range(copies):
            at = g * copies + copy
            for h in range(GROUP):
                part = slice(h * draft, (h + 1) * draft)
                out_ref[at, :, WIDE + h * HD : WIDE + (h + 1) * HD] = coarse[part].astype(BF16)
                out_ref[at, :, 2 * WIDE + h * HD : 2 * WIDE + (h + 1) * HD] = fine[part].astype(BF16)
                if copy == 0:
                    for t, term in enumerate((first, second, third)):
                        stats = jnp.where(stat_lane == 3 * h + t, term[part], stats)
            out_ref[at, :, 3 * WIDE :] = stats.astype(BF16)


def private_part(place, parents, lengths, queries, dkeys, dvals, pkeys, pvals, copies, batch):
    draft = queries.shape[0]
    slots = pkeys.shape[1]
    return pl.pallas_call(
        functools.partial(private_kernel, draft=draft, copies=copies, batch=batch),
        grid=(KVH // batch,),
        in_specs=[
            SMEM_SPEC,
            SMEM_SPEC,
            SMEM_SPEC,
            pl.BlockSpec((draft, batch * WIDE), lambda g: (0, g)),
            pl.BlockSpec((draft, batch * HD), lambda g: (0, g)),
            pl.BlockSpec((draft, batch * HD), lambda g: (0, g)),
            pl.BlockSpec((1, slots, batch * HD), lambda g: (0, 0, g)),
            pl.BlockSpec((1, slots, batch * HD), lambda g: (0, 0, g)),
        ],
        out_specs=pl.BlockSpec((batch * copies, draft, MESSAGE), lambda g: (g, 0, 0)),
        out_shape=jax.ShapeDtypeStruct((KVH * copies, draft, MESSAGE), BF16),
        compiler_params=pltpu.CompilerParams(vmem_limit_bytes=20 << 20),
        cost_estimate=pl.CostEstimate(
            flops=4 * draft * HEADS * slots * HD,
            transcendentals=draft * HEADS * slots,
            bytes_accessed=4 * slots * KVH * HD,
        ),
        name="private_part",
    )(place, parents, lengths, queries, dkeys, dvals, pkeys, pvals)


def stage_told(told_ref, told32, col, wide):
    chips, draft, _ = told_ref.shape
    for j in range(chips):
        part = slice(j * draft, (j + 1) * draft)
        told32[part, :wide] = told_ref[j, :, pl.ds(WIDE + col, wide)].astype(F32) + told_ref[
            j, :, pl.ds(2 * WIDE + col, wide)
        ].astype(F32)
        told32[part, wide:] = told_ref[j, :, 3 * WIDE :].astype(F32)


def merge_heads(out, lse, told32, att_ref, first_head):
    owned, wide = att_ref.shape
    stats = told32[:, wide:]
    lane = lax.broadcasted_iota(jnp.int32, (owned, LANES), 1)
    for h in range(wide // HD):
        at = 3 * (first_head + h)
        mark = (lane >= at) & (lane < at + 3)
        lse_p = jnp.sum(jnp.where(mark, stats, 0.0), axis=1, keepdims=True)
        part = slice(h * owned, (h + 1) * owned)
        lse_a = lse[part]
        top = jnp.maximum(lse_a, lse_p)
        scale_a = jnp.exp(lse_a - top)
        scale_p = jnp.exp(lse_p - top)
        mixed = scale_a * out[part] + scale_p * told32[:, h * HD : (h + 1) * HD]
        att_ref[:, h * HD : (h + 1) * HD] = (mixed / (scale_a + scale_p)).astype(BF16)


def prefix_kernel(
    place_ref,
    told_ref,
    k_ref,
    v_ref,
    twin_k_ref,
    twin_v_ref,
    w_ref,
    out_ref,
    wide_ref,
    told32,
    qs,
    peak,
    denom,
    acc,
    sem,
):
    step = pl.program_id(0)
    chips, draft, _ = told_ref.shape
    owned = chips * draft
    rows = owned * GROUP
    span = k_ref.shape[1]
    fetch = pltpu.make_async_copy(w_ref, wide_ref, sem)

    @pl.when(step == 2)
    def _():
        fetch.start()

    @pl.when(step == 0)
    def _():
        for j in range(chips):
            told32[j * draft : (j + 1) * draft, :WIDE] = told_ref[j, :, :WIDE].astype(F32)
        for h in range(GROUP):
            qs[h * owned : (h + 1) * owned, :] = told32[:, h * HD : (h + 1) * HD].astype(BF16)
        head = lax.dot_general(k_ref[0, :HD, :], qs[...], NT, preferred_element_type=F32)
        peak[...] = jnp.max(head, axis=0, keepdims=True) * (SCALE * LOG2E)
        denom[...] = jnp.zeros(denom.shape, F32)
        acc[...] = jnp.zeros(acc.shape, F32)

    keys = (k_ref[0], twin_k_ref[0])
    values = (v_ref[0], twin_v_ref[0])
    scores = [lax.dot_general(key, qs[...], NT, preferred_element_type=F32) for key in keys]
    weights = [jnp.exp2(score * (SCALE * LOG2E) - peak[...]) for score in scores]
    sums = [jnp.sum(weight.reshape(span // 8, 8, rows), axis=0) for weight in weights]
    mixes = [
        lax.dot_general(value, weight.astype(BF16), TN, preferred_element_type=F32)
        for value, weight in zip(values, weights)
    ]
    sums = [denom[i] + sums[i] for i in range(2)]
    mixes = [acc[i] + mixes[i] for i in range(2)]
    fits = jnp.max(jnp.maximum(sums[0], sums[1])) < LIMIT

    @pl.when(fits)
    def _():
        for i in range(2):
            denom[i] = sums[i]
            acc[i] = mixes[i]

    @pl.when(jnp.logical_not(fits))
    def _():
        part = 4 * HD

        def careful(i, keys, values):
            scores = lax.dot_general(keys, qs[...], NT, preferred_element_type=F32)
            scores = scores * (SCALE * LOG2E)
            old = peak[...]
            new = jnp.maximum(old, jnp.max(scores, axis=0, keepdims=True))
            fade = jnp.exp2(old - new)
            weights = jnp.exp2(scores - new)
            peak[...] = new
            sums = jnp.sum(weights.reshape(part // 8, 8, rows), axis=0)
            mixes = lax.dot_general(values, weights.astype(BF16), TN, preferred_element_type=F32)
            denom[i] = denom[i] * fade + sums
            acc[i] = acc[i] * fade + mixes
            denom[1 - i] = denom[1 - i] * fade
            acc[1 - i] = acc[1 - i] * fade

        @pl.loop(0, span // part)
        def _(b):
            block = pl.ds(pl.multiple_of(b * part, part), part)
            careful(0, k_ref[0, block, :], v_ref[0, block, :])
            careful(1, twin_k_ref[0, block, :], twin_v_ref[0, block, :])

    @pl.when(step == pl.num_programs(0) - 1)
    def _():
        total = jnp.sum(denom[0] + denom[1], axis=0, keepdims=True)
        lse = peak[...] * (1.0 / LOG2E) + jnp.log(total)
        mixed = ((acc[0] + acc[1]) / total).T
        lse = jnp.broadcast_to(lse, (LANES, rows)).T
        if out_ref.dtype == BF16:
            stage_told(told_ref, told32, 0, WIDE)
            merge_heads(mixed, lse, told32, out_ref, 0)
        else:
            out_ref[:, :HD] = mixed
            out_ref[:, HD:] = lse
        fetch.wait()


def prefix_part(place, told, keys, values, twin_keys, twin_values, weight, span, merged):
    chips, draft, _ = told.shape
    owned = chips * draft
    rows = owned * GROUP
    shape = jax.ShapeDtypeStruct((rows, HD + LANES), F32)
    if merged:
        shape = jax.ShapeDtypeStruct((owned, WIDE), BF16)
    return pl.pallas_call(
        prefix_kernel,
        grid=(keys.shape[1] // span,),
        in_specs=[
            SMEM_SPEC,
            pl.BlockSpec(told.shape, lambda i: (0, 0, 0)),
            pl.BlockSpec((1, span, HD), lambda i: (0, i, 0)),
            pl.BlockSpec((1, span, HD), lambda i: (0, i, 0)),
            pl.BlockSpec((1, span, HD), lambda i: (0, i, 0)),
            pl.BlockSpec((1, span, HD), lambda i: (0, i, 0)),
            pl.BlockSpec(memory_space=pl.ANY),
        ],
        out_specs=[pl.BlockSpec(shape.shape, lambda i: (0, 0)), VMEM_SPEC],
        out_shape=[
            shape,
            pltpu.VMEM(weight.shape, BF16),
        ],
        scratch_shapes=[
            pltpu.VMEM((owned, WIDE + LANES), F32),
            pltpu.VMEM((rows, HD), BF16),
            pltpu.VMEM((1, rows), F32),
            pltpu.VMEM((2, 8, rows), F32),
            pltpu.VMEM((2, HD, rows), F32),
            pltpu.SemaphoreType.DMA,
        ],
        compiler_params=pltpu.CompilerParams(vmem_limit_bytes=24 << 20),
        cost_estimate=pl.CostEstimate(
            flops=8 * rows * keys.shape[1] * HD,
            transcendentals=2 * rows * keys.shape[1],
            bytes_accessed=4 * keys.shape[1] * HD,
        ),
        name="prefix_part",
    )(
        place,
        on_chip(told),
        in_hbm(keys),
        in_hbm(values),
        on_chip(twin_keys),
        on_chip(twin_values),
        in_hbm(weight),
    )


def join(first, second):
    out_a, lse_a = first[:, :HD], first[:, HD:]
    out_b, lse_b = second[:, :HD], second[:, HD:]
    top = jnp.maximum(lse_a, lse_b)
    scale_a = jnp.exp(lse_a - top)
    scale_b = jnp.exp(lse_b - top)
    both = scale_a + scale_b
    return jnp.concatenate(
        [(scale_a * out_a + scale_b * out_b) / both, top + jnp.log(both)], axis=1
    )


def merge_kernel(place_ref, mine_ref, told_ref, att_ref, told32):
    wide = att_ref.shape[1]
    first_head = place_ref[2] * (wide // HD)
    stage_told(told_ref, told32, pl.multiple_of(first_head * HD, wide), wide)
    merge_heads(mine_ref[:, :HD], mine_ref[:, HD:], told32, att_ref, first_head)


def merge_part(place, mine, told):
    chips, draft, _ = told.shape
    owned = chips * draft
    wide = mine.shape[0] // owned * HD
    return pl.pallas_call(
        merge_kernel,
        in_specs=[SMEM_SPEC, VMEM_SPEC, VMEM_SPEC],
        out_specs=VMEM_SPEC,
        out_shape=pltpu.VMEM((owned, wide), BF16),
        scratch_shapes=[pltpu.VMEM((owned, wide + LANES), F32)],
        compiler_params=pltpu.CompilerParams(vmem_limit_bytes=8 << 20),
        cost_estimate=pl.CostEstimate(
            flops=8 * mine.size, transcendentals=mine.size, bytes_accessed=0
        ),
        name="merge_part",
    )(place, on_chip(mine), on_chip(told))


def project_kernel(place_ref, *refs, masks, first, last):
    part_ref, refs = (None, refs) if first else (refs[0], refs[1:])
    wide_ref, out_ref = refs[2 * len(masks) :]
    chip = place_ref[0]
    total = functools.reduce(
        jnp.add,
        [
            jnp.dot(
                jnp.concatenate([refs[2 * i][...], refs[2 * i + 1][...]], axis=0),
                wide_ref[chip ^ mask],
                preferred_element_type=F32,
            )
            for i, mask in enumerate(masks)
        ],
    )
    if not first:
        total = total + part_ref[...]
    if not last:
        out_ref[...] = total
        return
    owners, draft, _ = out_ref.shape
    half = owners // 2 * draft
    own, twin = total[:half], total[half:]
    even = place_ref[1] == 0
    halves = (jnp.where(even, own, twin), jnp.where(even, twin, own))
    for s in range(owners):
        at = s // 2 * draft
        out_ref[s] = halves[s % 2][at : at + draft].astype(BF16)


def project(place, part, chunks, wide, owners, last):
    masks = tuple(chunks)
    rows, deep = chunks[masks[0]][0].shape
    cols = wide.shape[2]
    first = part is None
    arrays = [] if first else [part]
    for mask in masks:
        arrays.extend(chunks[mask])
    arrays.append(wide)
    shape = (owners, 2 * rows // owners, cols) if last else (2 * rows, cols)
    return pl.pallas_call(
        functools.partial(project_kernel, masks=masks, first=first, last=last),
        in_specs=[SMEM_SPEC] + [VMEM_SPEC] * len(arrays),
        out_specs=VMEM_SPEC,
        out_shape=pltpu.VMEM(shape, BF16 if last else F32),
        compiler_params=pltpu.CompilerParams(vmem_limit_bytes=8 << 20),
        cost_estimate=pl.CostEstimate(
            flops=4 * rows * deep * len(masks) * cols, transcendentals=0, bytes_accessed=0
        ),
        name="project_last" if last else "project",
    )(place, *[on_chip(array) for array in arrays])


def shards(
    queries,
    draft_keys,
    draft_values,
    parents,
    private_keys,
    private_values,
    priv_lengths,
    prefix_keys,
    prefix_values,
    out_weight,
):
    own_rows = queries.shape[0]
    seq = lax.axis_size("seq")
    chips = seq // 2
    blocks = seq // KVH
    device = lax.axis_index("seq")
    chip = device // 2
    sharers = blocks // 2
    rank = chip % sharers
    place = jnp.stack([chip, device % 2, rank]).astype(jnp.int32)
    members = [list(range(c, seq, 2)) for c in range(2)]

    def from_partner(array, mask):
        return lax.ppermute(array, "seq", [(i, i ^ mask) for i in range(seq)])

    twin_keys = from_partner(prefix_keys, 1)
    twin_values = from_partner(prefix_values, 1)
    message = private_part(
        place,
        in_hbm(parents),
        priv_lengths,
        in_hbm(queries),
        in_hbm(draft_keys),
        in_hbm(draft_values),
        in_hbm(private_keys),
        in_hbm(private_values),
        sharers,
        KVH // 2,
    )
    told = lax.all_to_all(
        message, "seq", split_axis=0, concat_axis=0, axis_index_groups=members, tiled=True
    )

    span = min((1 << 20) // (chips * own_rows * GROUP), prefix_keys.shape[1])
    weight = out_weight.reshape(chips, -1, out_weight.shape[1])
    mine, wide = prefix_part(
        place, told, prefix_keys, prefix_values, twin_keys, twin_values, weight, span, sharers == 1
    )
    for level in range(sharers.bit_length() - 2, -1, -1):
        half = mine.shape[0] // 2
        at = (rank >> level) & 1
        kept = lax.dynamic_slice_in_dim(mine, at * half, half, 0)
        gone = lax.dynamic_slice_in_dim(mine, (1 - at) * half, half, 0)
        mine = join(kept, from_partner(gone, 2 << level))

    own = {0: mine if sharers == 1 else merge_part(place, mine, told)}
    twin = {}
    far = [2 * k for k in range(1, chips // 2)]

    def move(target, mask, source, step):
        target[mask] = from_partner(source, step)

    for mask in [1] + far:
        move(own, mask, own[0], 2 * mask)
    for mask in far:
        move(own, mask + 1, own[mask], 2)
    for mask in own:
        move(twin, mask, own[mask], 1)
    stages = [[0] + far[:-1], [1, far[-1]] + [m + 1 for m in far[:-1]], [far[-1] + 1]]
    part = None
    for number, stage in enumerate(stages):
        chunks = {mask: (own[mask], twin[mask]) for mask in stage}
        part = project(place, part, chunks, wide, seq, number == len(stages) - 1)
    pieces = part
    done = lax.all_to_all(pieces, "seq", split_axis=0, concat_axis=0, tiled=True)
    return done.transpose(1, 0, 2).reshape(own_rows, -1).astype(F32)


def solution(mesh):
    in_specs = (
        P(("groups", "seq"), None),
        P(("groups", "seq"), None),
        P(("groups", "seq"), None),
        P(("groups", "seq")),
        P(("groups", "seq"), None, None),
        P(("groups", "seq"), None, None),
        P(("groups", "seq")),
        P(("groups", "seq"), None, None),
        P(("groups", "seq"), None, None),
        P(None, "seq"),
    )
    out_specs = P(("groups", "seq"), None)

    return jax.shard_map(shards, mesh=mesh, in_specs=in_specs, out_specs=out_specs, check_vma=False)
```
